32 devices in a mesh: pipe: 2 (over y), dp: 16 (over z, x, core).
Axes of the slice: x: 2, y: 2, z: 4, core: 2. Of those that a mesh axis runs over, the one named last changes fastest.
Arguments:
- layer_inputs: bfloat16 [2, 16, 2, 64, 2560], P('pipe', 'dp'), may hold values from -6 to 6
- top_grad: bfloat16 [16, 2, 64, 2560], P('dp'), may hold values from -6 to 6
- keys: bfloat16 [2, 16, 1024, 512], P('pipe', 'dp'), may hold values from -250 to 250
- values: bfloat16 [2, 16, 1024, 512], P('pipe', 'dp'), may hold values from -6 to 6
- query_weight: bfloat16 [2, 2560, 2560], P('pipe', 'dp'), may hold values from -0.125 to 0.125
- adapter_a: bfloat16 [2, 2560, 32], P('pipe', 'dp'), may hold values from -0.125 to 0.125
- adapter_bt: bfloat16 [2, 2560, 32], P('pipe', 'dp'), may hold values from -0.125 to 0.125
- norm_gain: bfloat16 [2, 2560], P('pipe', 'dp'), may hold values from 0.5 to 1.5
- offsets: int32 [16, 2], P('dp'), may hold values from 0 to 960, as said below
- segments: int32 [16, 1024], P('dp'), may hold values from 0 to 10, as said below
Outputs:
- section_grads: bfloat16 [2, 16, 2, 64, 2560], P('pipe', 'dp')
- grad_a: float32 [2, 2560, 32], P('pipe', 'dp')
- grad_bt: float32 [2, 2560, 32], P('pipe', 'dp')
The draws below stay inside these ranges and needn't reach their ends.
Inputs may be any that keep to these rules, and one draw needn't show every extreme that they name: `offsets`: each offset is a multiple of 64. `segments`: segment 0 is the schema and covers positions 0 up to a length of at least 256; the numbers never fall along a sequence.
All inputs are finite; a program needn't handle non-finite values.
Results may differ from the reference program's by a relative error of at most 0.03.
The reference program's roundings to bfloat16 on the way count: a program that leaves them out, or rounds other values in their place, can miss the bound.
Values may be sent and summed in bfloat16 or wider, within the bound.
No kernel may reach another device: no remote copies, remote signals or barrier semaphores. Data moves between devices by JAX's collectives and lax.ppermute only.
A program may use at most 128 MiB of HBM per device.

```python
import jax
import jax.numpy as jnp
from jax import lax

D = 2560
HEADS = 20
KV_HEADS = 4
HEAD_DIM = 128
RANK = 32
MICRO = 2
MB_TOK = 64
CTX = 1024
QW = 2560
KVW = 512
BATCH = 16
SECTIONS = 2
N_PIPE = 2


def draw_keys(key, part):
    shape = (N_PIPE, BATCH, CTX, KV_HEADS * HEAD_DIM)
    first_key = jax.random.fold_in(jax.random.fold_in(key, 11), 0)
    result = 2.0 * jnp.clip(jax.random.normal(first_key, shape, jnp.float32), -6.0, 6.0)
    return result.astype(jnp.bfloat16)


def draw_offsets(key, part):
    blocks = jax.random.randint(jax.random.fold_in(key, 23), (BATCH, MICRO), 0, CTX // MB_TOK)
    return (blocks * MB_TOK).astype(jnp.int32)


def draw_segments(key, part):
    first_key, second_key = jax.random.split(jax.random.fold_in(key, 37), 2)
    top_number = 2 + CTX // 128
    schema = CTX // 4 + jax.random.randint(first_key, (BATCH, 1), 0, CTX // 4 + 1)
    place = jnp.arange(CTX, dtype=jnp.int32)[None, :]
    starts = (jax.random.randint(second_key, (BATCH, CTX), 0, 48) == 0) & (place > schema)
    numbers = jnp.minimum(1 + jnp.cumsum(starts.astype(jnp.int32), axis=1), top_number)
    numbers = jnp.where(place >= CTX - CTX // 16, top_number, numbers)
    return jnp.where(place >= schema, numbers, 0).astype(jnp.int32)


def spiked(values, own_key, source, target, blocks, factor):
    def block_of(position):
        return (jnp.arange(values.shape[position]) // (values.shape[position] // blocks)).reshape((-1,) + (1,) * (values.ndim - 1 - position))

    first = jax.random.permutation(own_key, blocks)[block_of(target)]
    far = (block_of(target) + blocks // 2) % blocks
    return jnp.where((block_of(source) == first) | (block_of(source) == far), factor * values, values)


def block_levels(own_key, dims, cuts, least, high):
    level, own = 1.0, jax.random.fold_in(own_key, 6)
    for axis_at, parts in cuts:
        steps = jnp.exp(jax.random.uniform(jax.random.fold_in(own, axis_at), (parts,), jnp.float32, least / len(cuts), high / len(cuts)))
        level = level * jnp.repeat(steps, dims[axis_at] // parts).reshape([-1 if axis == axis_at else 1 for axis in range(len(dims))])
    return level


def normal_values(own_key, extent, scale, reach, cuts=(), kind=jnp.bfloat16):
    values = jax.random.normal(own_key, extent, jnp.float32) * scale
    if len(cuts) > 0:
        values = block_levels(own_key, extent, cuts, -0.22, 0.18) * values
    return jnp.clip(values, min=-reach, max=reach).astype(kind)


def heavy_noise(key, dims, deviation, most, cuts, heavy, kind=jnp.bfloat16):
    values = deviation * jax.random.normal(key, dims, jnp.float32)
    if cuts:
        values = values * block_levels(key, dims, cuts, -0.22, 0.18)
    return jnp.clip(spiked(values, jax.random.fold_in(key, 3), *heavy), -most, most).astype(kind)


def setup_inputs(seed: int = 0) -> dict:
    streams_of = jax.random.split(jax.random.key(seed), 11)
    return {
        "layer_inputs": heavy_noise(streams_of[0], (SECTIONS, BATCH, MICRO, MB_TOK, D), 1.0, 6.0, ((0, 2), (1, 16)), (1, 4, 16, 2.0)),
        "top_grad": normal_values(streams_of[1], (BATCH, MICRO, MB_TOK, D), 1.0, 6.0, ((0, 16),)),
        "keys": draw_keys(jax.random.fold_in(streams_of[10], 71), 0),
        "values": normal_values(streams_of[3], (SECTIONS, BATCH, CTX, KVW), 1.0, 6.0, ((0, 2), (1, 16))),
        "query_weight": normal_values(streams_of[4], (SECTIONS, D, QW), D ** -0.5, 0.125, ((0, 2), (1, 16))),
        "adapter_a": normal_values(streams_of[5], (SECTIONS, D, RANK), D ** -0.5, 0.125, ((0, 2), (1, 16))),
        "adapter_bt": normal_values(streams_of[6], (SECTIONS, QW, RANK), QW ** -0.5, 0.125, ((0, 2), (1, 16))),
        "norm_gain": jnp.clip(1.0 + 0.1 * jax.random.normal(streams_of[7], (SECTIONS, D), jnp.float32), 0.5, 1.5).astype(jnp.bfloat16),
        "offsets": draw_offsets(jax.random.fold_in(streams_of[10], 71), 0),
        "segments": draw_segments(jax.random.fold_in(streams_of[10], 71), 0),
    }


norm_eps = 1e-06
rope_base = 1000000.0

def rope_tables(positions, head_dim):
    half = head_dim // 2
    expon = jnp.arange(half, dtype=jnp.float32) * (2.0 / head_dim)
    inverse = rope_base ** (-expon)
    angles = positions.astype(jnp.float32)[:, None] * inverse[None, :]
    return (jnp.cos(angles)[:, None, :], jnp.sin(angles)[:, None, :])

def rotate(query, cosine, sine):
    half = query.shape[-1] // 2
    first = query[..., :half]
    second = query[..., half:]
    return jnp.concatenate([first * cosine - second * sine, second * cosine + first * sine], axis=-1)

def unrotate(grad, cosine, sine):
    half = grad.shape[-1] // 2
    first = grad[..., :half]
    second = grad[..., half:]
    return jnp.concatenate([first * cosine + second * sine, second * cosine - first * sine], axis=-1)

def round_half(value):
    return lax.optimization_barrier(value.astype(jnp.bfloat16)).astype(jnp.float32)

def section_backward(rows_in, upstream_gradient, keys_one, values_one, positions, seg_row, weight, factor_a, factor_bt, gain):
    count = rows_in.shape[0]
    group = HEADS // KV_HEADS
    flattened_rows = rows_in.astype(jnp.float32)
    reciprocal_norm = lax.rsqrt(lax.optimization_barrier(jnp.mean(flattened_rows * flattened_rows, axis=1, keepdims=True)) + norm_eps)
    normalized_values = flattened_rows * reciprocal_norm
    broadcast_gain = gain.astype(jnp.float32)
    normalized_input = (normalized_values * broadcast_gain[None, :]).astype(jnp.bfloat16)
    lowrank = jnp.dot(normalized_input, factor_a, preferred_element_type=jnp.float32).astype(jnp.bfloat16)
    query = jnp.dot(normalized_input, weight, preferred_element_type=jnp.float32) + jnp.dot(lowrank, factor_bt.T, preferred_element_type=jnp.float32)
    cosine, sine = rope_tables(positions, HEAD_DIM)
    rotated = rotate(query.reshape(count, HEADS, HEAD_DIM), cosine, sine).astype(jnp.bfloat16)
    ctx_len = seg_row.shape[0]
    place = jnp.arange(ctx_len, dtype=jnp.int32)
    query_seg = jnp.take(seg_row, positions)
    visible = (place[None, :] <= positions[:, None]) & ((seg_row[None, :] == 0) | (seg_row[None, :] == query_seg[:, None]))
    keys_heads = keys_one.reshape(ctx_len, KV_HEADS, HEAD_DIM).astype(jnp.float32)
    values_heads = values_one.reshape(ctx_len, KV_HEADS, HEAD_DIM).astype(jnp.float32)
    grouped = rotated.reshape(count, KV_HEADS, group, HEAD_DIM).astype(jnp.float32)
    grad_heads = upstream_gradient.reshape(count, KV_HEADS, group, HEAD_DIM).astype(jnp.float32)
    scale = 1.0 / HEAD_DIM ** 0.5
    scores = jnp.einsum('nhgd,chd->nhgc', grouped, keys_heads) * scale
    scores = jnp.where(visible[:, None, None, :], scores, -1e+30)
    highest = lax.optimization_barrier(jnp.max(scores, axis=-1, keepdims=True))
    expo = jnp.exp(scores - highest)
    probs = expo / lax.optimization_barrier(jnp.sum(expo, axis=-1, keepdims=True))
    probs_b = round_half(probs)
    attended = jnp.einsum('nhgc,chd->nhgd', probs_b, values_heads)
    dprobs = jnp.einsum('nhgd,chd->nhgc', grad_heads, values_heads)
    delta = lax.optimization_barrier(jnp.sum(grad_heads * attended, axis=-1, keepdims=True))
    dscores = round_half(probs * (dprobs - delta) * scale)
    drot = jnp.einsum('nhgc,chd->nhgd', dscores, keys_heads).reshape(count, HEADS, HEAD_DIM)
    dquery = unrotate(drot, cosine, sine).reshape(count, HEADS * HEAD_DIM).astype(jnp.bfloat16)
    mid = jnp.dot(dquery, factor_bt, preferred_element_type=jnp.float32).astype(jnp.bfloat16)
    dnormed = jnp.dot(dquery, weight.T, preferred_element_type=jnp.float32) + jnp.dot(mid, factor_a.T, preferred_element_type=jnp.float32)
    normalized_gradient = dnormed * broadcast_gain[None, :]
    input_gradient = upstream_gradient.astype(jnp.float32) + reciprocal_norm * (normalized_gradient - normalized_values * lax.optimization_barrier(jnp.mean(normalized_gradient * normalized_values, axis=1, keepdims=True)))
    grad_a = jnp.dot(normalized_input.T, mid, preferred_element_type=jnp.float32)
    grad_bt = jnp.dot(dquery.T, lowrank, preferred_element_type=jnp.float32)
    return (input_gradient.astype(jnp.bfloat16), grad_a, grad_bt)

def reference(layer_inputs, top_grad, keys, values, query_weight, adapter_a, adapter_bt, norm_gain, offsets, segments):
    upstream_gradient = top_grad
    grads_list = [None] * N_PIPE
    a_list = [None] * N_PIPE
    bt_list = [None] * N_PIPE
    for level in range(N_PIPE - 1, -1, -1):

        def per_sequence(operands):
            rows_in, grad_rows, keys_one, values_one, starts, seg_row = operands
            positions = (starts[:, None] + jnp.arange(MB_TOK, dtype=jnp.int32)[None, :]).reshape(MICRO * MB_TOK)
            input_gradient, grad_a, grad_bt = section_backward(rows_in.reshape(MICRO * MB_TOK, D), grad_rows.reshape(MICRO * MB_TOK, D), keys_one, values_one, positions, seg_row, query_weight[level], adapter_a[level], adapter_bt[level], norm_gain[level])
            return (input_gradient.reshape(MICRO, MB_TOK, D), grad_a, grad_bt)
        input_gradient, grad_a, grad_bt = lax.map(per_sequence, (layer_inputs[level], upstream_gradient, keys[level], values[level], offsets, segments))
        grads_list[level] = input_gradient
        a_list[level] = lax.optimization_barrier(jnp.sum(grad_a, axis=0))
        bt_list[level] = lax.optimization_barrier(jnp.sum(grad_bt, axis=0))
        upstream_gradient = input_gradient
    return (jnp.stack(grads_list), jnp.stack(a_list), jnp.stack(bt_list))
```

```python
import jax
import jax.numpy as jnp
from jax import lax
from jax.experimental import pallas as pl
from jax.experimental.pallas import tpu as pltpu
from jax.sharding import PartitionSpec as P

HEADS = 20
KV_HEADS = 4
HEAD_DIM = 128
GROUP = HEADS // KV_HEADS

norm_eps = 1e-06
rope_base = 1000000.0
SCALE = 1.0 / HEAD_DIM**0.5

NT = (((1,), (1,)), ((), ()))
TN = (((0,), (0,)), ((), ()))


def dot(a, b, dims=(((1,), (0,)), ((), ()))):
    return lax.dot_general(a, b, dims, preferred_element_type=jnp.float32)


def rope_tables(positions):
    half = HEAD_DIM // 2
    expon = jnp.arange(half, dtype=jnp.float32) * (2.0 / HEAD_DIM)
    inverse = rope_base ** (-expon)
    angles = positions.astype(jnp.float32)[:, None] * inverse[None, :]
    cosine, sine = jnp.cos(angles), jnp.sin(angles)
    return (
        jnp.concatenate([cosine, cosine], axis=1),
        jnp.concatenate([-sine, sine], axis=1),
    )


def query_kernel(normed, lowrank, weight, factor_bt, cosine, sine, rotated):
    query = dot(normed[...], weight[...]) + dot(lowrank[...], factor_bt[...], NT)
    for j in range(GROUP):
        part = query[:, j * HEAD_DIM : (j + 1) * HEAD_DIM]
        turned = part * cosine[...] + pltpu.roll(part, HEAD_DIM // 2, 1) * sine[...]
        rotated[:, j * HEAD_DIM : (j + 1) * HEAD_DIM] = turned.astype(jnp.bfloat16)


def project(normed, lowrank, weight, factor_bt, cosine, sine):
    rows, width = normed.shape
    features = weight.shape[1]
    rank = lowrank.shape[1]
    block = features // KV_HEADS
    return pl.pallas_call(
        query_kernel,
        grid=(KV_HEADS,),
        in_specs=[
            pl.BlockSpec((rows, width), lambda h: (0, 0)),
            pl.BlockSpec((rows, rank), lambda h: (0, 0)),
            pl.BlockSpec((width, block), lambda h: (0, h)),
            pl.BlockSpec((block, rank), lambda h: (h, 0)),
            pl.BlockSpec((rows, HEAD_DIM), lambda h: (0, 0)),
            pl.BlockSpec((rows, HEAD_DIM), lambda h: (0, 0)),
        ],
        out_specs=pl.BlockSpec((rows, block), lambda h: (0, h)),
        out_shape=jax.ShapeDtypeStruct((rows, features), jnp.bfloat16),
        name="project",
    )(normed, lowrank, weight, factor_bt, cosine, sine)


def backward_kernel(
    micro,
    rotated,
    upstream,
    keys,
    values,
    bias,
    cosine,
    sine,
    weight,
    factor_bt,
    factor_a,
    rows_in,
    reciprocal,
    gain,
    kept_dquery,
    kept_middle,
    input_gradient,
    dquery,
    middle,
    total,
    middle_sum,
):
    h = pl.program_id(0)
    block = GROUP * HEAD_DIM
    for j in range(GROUP):
        at = slice(j * HEAD_DIM, (j + 1) * HEAD_DIM)
        where = pl.ds(pl.multiple_of(h * block + j * HEAD_DIM, HEAD_DIM), HEAD_DIM)
        scores = dot(rotated[0, :, at], keys[...], NT) * SCALE + bias[0]
        highest = jnp.max(scores, axis=-1, keepdims=True)
        expo = jnp.exp(scores - highest)
        probs = expo * (1.0 / jnp.sum(expo, axis=-1, keepdims=True))
        rounded = probs.astype(jnp.bfloat16).astype(jnp.float32)
        dprobs = dot(upstream[:, where], values[...], NT)
        delta = jnp.sum(rounded * dprobs, axis=-1, keepdims=True)
        dscores = (probs * (dprobs - delta) * SCALE).astype(jnp.bfloat16)
        drot = dot(dscores, keys[...])
        turned = drot * cosine[0] - pltpu.roll(drot, HEAD_DIM // 2, 1) * sine[0]
        dquery[0, :, at] = turned.astype(jnp.bfloat16)
    mine = dquery[0]
    part = dot(mine, weight[...], NT)
    low = dot(mine, factor_bt[...])

    @pl.when(h == 0)
    def _():
        total[...] = part
        middle_sum[...] = low

    @pl.when(h > 0)
    def _():
        total[...] += part
        middle_sum[...] += low

    @pl.when(h == pl.num_programs(0) - 1)
    def _():
        mid = middle_sum[...].astype(jnp.bfloat16)
        middle[0] = mid
        dh = (total[...] + dot(mid, factor_a[...], NT)) * gain[...]
        scaled = rows_in[0].astype(jnp.float32) * reciprocal[0]
        mean = jnp.mean(dh * scaled, axis=1, keepdims=True)
        result = upstream[...].astype(jnp.float32) + reciprocal[0] * (dh - scaled * mean)
        input_gradient[...] = result.astype(jnp.bfloat16)


def backward(
    micro,
    rotated,
    upstream,
    keys,
    values,
    bias,
    cosine,
    sine,
    weight,
    factor_bt,
    factor_a,
    rows_in,
    reciprocal,
    gain,
    kept,
):
    micros, tokens, features = rotated.shape
    width = weight.shape[0]
    rank = factor_a.shape[1]
    ctx = keys.shape[0]
    block = features // KV_HEADS
    whole = lambda *dims: pl.BlockSpec(dims, lambda h, m: (0,) * len(dims))
    of_micro = lambda *dims: pl.BlockSpec(
        (1, *dims), lambda h, m: (m[0],) + (0,) * len(dims)
    )
    untouched = pl.BlockSpec(memory_space=pl.ANY)
    return pl.pallas_call(
        backward_kernel,
        grid_spec=pltpu.PrefetchScalarGridSpec(
            num_scalar_prefetch=1,
            grid=(KV_HEADS,),
            in_specs=[
                pl.BlockSpec((1, tokens, block), lambda h, m: (m[0], 0, h)),
                whole(tokens, features),
                pl.BlockSpec((ctx, HEAD_DIM), lambda h, m: (0, h)),
                pl.BlockSpec((ctx, HEAD_DIM), lambda h, m: (0, h)),
                of_micro(tokens, ctx),
                of_micro(tokens, HEAD_DIM),
                of_micro(tokens, HEAD_DIM),
                pl.BlockSpec((width, block), lambda h, m: (0, h)),
                pl.BlockSpec((block, rank), lambda h, m: (h, 0)),
                whole(width, rank),
                of_micro(tokens, width),
                of_micro(tokens, 1),
                whole(1, width),
                untouched,
                untouched,
            ],
            out_specs=[
                whole(tokens, width),
                pl.BlockSpec((1, tokens, block), lambda h, m: (m[0], 0, h)),
                of_micro(tokens, rank),
            ],
            scratch_shapes=[
                pltpu.VMEM((tokens, width), jnp.float32),
                pltpu.VMEM((tokens, rank), jnp.float32),
            ],
        ),
        out_shape=[
            jax.ShapeDtypeStruct((tokens, width), jnp.bfloat16),
            jax.ShapeDtypeStruct((micros, tokens, features), jnp.bfloat16),
            jax.ShapeDtypeStruct((micros, tokens, rank), jnp.bfloat16),
        ],
        input_output_aliases={14: 1, 15: 2},
        name="backward",
    )(
        micro,
        rotated,
        upstream,
        keys,
        values,
        bias,
        cosine,
        sine,
        weight,
        factor_bt,
        factor_a,
        rows_in,
        reciprocal,
        gain,
        *kept,
    )


def gather_small(adapter_a, adapter_bt, norm_gain):
    count = lax.axis_size("dp")
    share, rank = adapter_a.shape
    packed = jnp.concatenate([adapter_a, adapter_bt, norm_gain[:, None]], axis=1)
    sent = jnp.broadcast_to(packed[None], (count, *packed.shape))
    got = lax.all_to_all(sent, "dp", split_axis=0, concat_axis=0, tiled=True)
    got = got.reshape(count * share, 2 * rank + 1)
    return got[:, :rank], got[:, rank : 2 * rank], got[:, 2 * rank]


def summed_shares(grad_a, grad_bt):
    count = lax.axis_size("dp")
    width, rank = grad_a.shape
    share = width // count
    both = jnp.concatenate([grad_a, grad_bt], axis=1).reshape(count, share, 2 * rank)
    packed = jnp.concatenate([both[:, : share // 2], both[:, share // 2 :]], axis=2)
    got = lax.all_to_all(packed, "dp", split_axis=0, concat_axis=0, tiled=True)
    total = jnp.sum(got, axis=0)
    total = jnp.concatenate([total[:, : 2 * rank], total[:, 2 * rank :]], axis=0)
    return total[:, :rank], total[:, rank:]


def per_device(
    layer_inputs,
    top_grad,
    keys,
    values,
    query_weight,
    adapter_a,
    adapter_bt,
    norm_gain,
    offsets,
    segments,
):
    rows_in = layer_inputs[0, 0]
    micros, tokens, width = rows_in.shape
    rows = micros * tokens
    ctx = keys.shape[2]
    keys, values = keys[0, 0], values[0, 0]
    features = query_weight.shape[2]

    weight = lax.all_gather(query_weight[0], "dp", axis=0, tiled=True)
    factor_a, factor_bt, gain = gather_small(adapter_a[0], adapter_bt[0], norm_gain[0])

    flat = rows_in.reshape(rows, width).astype(jnp.float32)
    reciprocal = lax.rsqrt(jnp.mean(flat * flat, axis=1, keepdims=True) + norm_eps)
    gain = gain.astype(jnp.float32)[None, :]
    normed = (flat * reciprocal * gain).astype(jnp.bfloat16)
    lowrank = dot(normed, factor_a).astype(jnp.bfloat16)

    positions = (
        offsets[0][:, None] + jnp.arange(tokens, dtype=jnp.int32)[None, :]
    ).reshape(rows)
    seg_row = segments[0]
    place = jnp.arange(ctx, dtype=jnp.int32)
    query_seg = jnp.take(seg_row, positions)
    visible = (place[None, :] <= positions[:, None]) & (
        (seg_row[None, :] == 0) | (seg_row[None, :] == query_seg[:, None])
    )
    bias = jnp.where(visible, 0.0, -1e30).astype(jnp.float32)
    cosine, sine = rope_tables(positions)

    rotated = project(normed, lowrank, weight, factor_bt, cosine, sine)

    by_micro = lambda a: a.reshape(micros, tokens, a.shape[-1])
    section_count = lax.axis_size("pipe")
    section = lax.axis_index("pipe")
    last = section_count - 1
    kept = (
        jnp.zeros((micros, tokens, features), jnp.bfloat16),
        jnp.zeros((micros, tokens, adapter_a.shape[2]), jnp.bfloat16),
    )
    results = []
    incoming = None
    for step in range(section_count + micros - 1):
        micro = jnp.clip(step - (last - section), 0, micros - 1)
        own = top_grad[0, min(step, micros - 1)]
        upstream = own if step == 0 else jnp.where(section == last, own, incoming)
        result, *kept = backward(
            micro.reshape(1).astype(jnp.int32),
            by_micro(rotated),
            upstream,
            keys,
            values,
            by_micro(bias),
            by_micro(cosine),
            by_micro(sine),
            weight,
            factor_bt,
            factor_a,
            rows_in,
            by_micro(reciprocal),
            gain,
            kept,
        )
        results.append(result)
        if step < section_count + micros - 2:
            incoming = lax.ppermute(
                result, "pipe", [(s, s - 1) for s in range(1, section_count)]
            )

    def of_micro(m):
        chosen = results[m]
        for back in range(1, section_count):
            chosen = jnp.where(last - section == back, results[m + back], chosen)
        return chosen

    grads = jnp.stack([of_micro(m) for m in range(micros)])
    dquery = kept[0].reshape(rows, features)
    middle = kept[1].reshape(rows, -1)
    share_a, share_bt = summed_shares(dot(normed, middle, TN), dot(dquery, lowrank, TN))
    return (grads[None, None], share_a[None], share_bt[None])


def solution(mesh):
    placed = (
        P("pipe", "dp", None, None, None),
        P("dp", None, None, None),
        P("pipe", "dp", None, None),
        P("pipe", "dp", None, None),
        P("pipe", "dp", None),
        P("pipe", "dp", None),
        P("pipe", "dp", None),
        P("pipe", "dp"),
        P("dp", None),
        P("dp", None),
    )
    return jax.shard_map(
        per_device,
        mesh=mesh,
        in_specs=placed,
        out_specs=(
            P("pipe", "dp", None, None, None),
            P("pipe", "dp", None),
            P("pipe", "dp", None),
        ),
        check_vma=False,
    )
```

```python
import functools

import jax
import jax.numpy as jnp
from jax import lax
from jax.experimental import pallas as pl
from jax.experimental.pallas import tpu as pltpu
from jax.sharding import PartitionSpec as P

HEADS = 20
KV_HEADS = 4
HEAD_DIM = 128
GROUP = HEADS // KV_HEADS

norm_eps = 1e-06
rope_base = 1000000.0
SCALE = 1.0 / HEAD_DIM**0.5

NT = (((1,), (1,)), ((), ()))
TN = (((0,), (0,)), ((), ()))


def dot(a, b, dims=(((1,), (0,)), ((), ()))):
    return lax.dot_general(a, b, dims, preferred_element_type=jnp.float32)


def rope_tables(positions):
    half = HEAD_DIM // 2
    expon = jnp.arange(half, dtype=jnp.float32) * (2.0 / HEAD_DIM)
    inverse = rope_base ** (-expon)
    angles = positions.astype(jnp.float32)[:, None] * inverse[None, :]
    cosine, sine = jnp.cos(angles), jnp.sin(angles)
    return (
        jnp.concatenate([cosine, cosine], axis=1),
        jnp.concatenate([-sine, sine], axis=1),
    )


def query_kernel(normed, lowrank, weight, factor_bt, cosine, sine, rotated):
    query = dot(normed[...], weight[...]) + dot(lowrank[...], factor_bt[...], NT)
    for j in range(GROUP):
        part = query[:, j * HEAD_DIM : (j + 1) * HEAD_DIM]
        turned = part * cosine[...] + pltpu.roll(part, HEAD_DIM // 2, 1) * sine[...]
        rotated[:, j * HEAD_DIM : (j + 1) * HEAD_DIM] = turned.astype(jnp.bfloat16)


def project(normed, lowrank, weight, factor_bt, cosine, sine):
    rows, width = normed.shape
    features = weight.shape[1]
    rank = lowrank.shape[1]
    block = features // KV_HEADS
    return pl.pallas_call(
        query_kernel,
        grid=(KV_HEADS,),
        in_specs=[
            pl.BlockSpec((rows, width), lambda h: (0, 0)),
            pl.BlockSpec((rows, rank), lambda h: (0, 0)),
            pl.BlockSpec((width, block), lambda h: (0, h)),
            pl.BlockSpec((block, rank), lambda h: (h, 0)),
            pl.BlockSpec((rows, HEAD_DIM), lambda h: (0, 0)),
            pl.BlockSpec((rows, HEAD_DIM), lambda h: (0, 0)),
        ],
        out_specs=pl.BlockSpec((rows, block), lambda h: (0, h)),
        out_shape=jax.ShapeDtypeStruct((rows, features), jnp.bfloat16),
        name="project",
    )(normed, lowrank, weight, factor_bt, cosine, sine)


def ring_order(count):
    if count % 4:
        return list(range(count))
    chips = count // 2
    columns = 2 ** ((chips.bit_length() - 1) // 2)
    lines = chips // columns
    walk = [(z, 0) for z in range(lines)]
    for step, z in enumerate(range(lines - 1, -1, -1)):
        side = range(1, columns) if step % 2 == 0 else range(columns - 1, 0, -1)
        walk += [(z, x) for x in side]
    return [(z * columns + x) * 2 + core for z, x in walk for core in range(2)]


def reordered(value, order):
    share = value.shape[-1] // len(order)
    return jnp.concatenate(
        [value[..., i * share : (i + 1) * share] for i in order], axis=-1
    )


def stacked(value):
    return jnp.concatenate(
        [value[:, j * HEAD_DIM : (j + 1) * HEAD_DIM] for j in range(GROUP)], axis=0
    )


def backward_kernel(
    order,
    micro,
    rotated,
    upstream,
    keys,
    values,
    bias,
    cosine,
    sine,
    weight,
    factor_bt,
    factor_a,
    rows_in,
    reciprocal,
    gain,
    *rest,
):
    input_gradient, dquery, middle, total, middle_sum = rest[-5:]
    h = pl.program_id(0)
    tokens = bias.shape[1]
    block = GROUP * HEAD_DIM
    mine = pl.ds(pl.multiple_of(h * block, HEAD_DIM), block)
    scores = dot(stacked(rotated[0]), keys[...], NT)
    dprobs = dot(stacked(upstream[:, mine]), values[...], NT)
    dscores = []
    for j in range(GROUP):
        at = slice(j * tokens, (j + 1) * tokens)
        masked = scores[at] * SCALE + bias[0]
        expo = jnp.exp(masked - jnp.max(masked, axis=-1, keepdims=True))
        probs = expo * (1.0 / jnp.sum(expo, axis=-1, keepdims=True))
        rounded = probs.astype(jnp.bfloat16).astype(jnp.float32)
        delta = jnp.sum(rounded * dprobs[at], axis=-1, keepdims=True)
        dscores.append((probs * (dprobs[at] - delta) * SCALE).astype(jnp.bfloat16))
    drot = dot(jnp.concatenate(dscores, axis=0), keys[...])
    for j in range(GROUP):
        part = drot[j * tokens : (j + 1) * tokens]
        turned = part * cosine[0] - pltpu.roll(part, HEAD_DIM // 2, 1) * sine[0]
        dquery[0, :, j * HEAD_DIM : (j + 1) * HEAD_DIM] = turned.astype(jnp.bfloat16)
    dq = dquery[0]
    part = dot(dq, weight[...], NT)
    low = dot(dq, factor_bt[...])

    @pl.when(h == 0)
    def _():
        total[...] = part
        middle_sum[...] = low

    @pl.when(h > 0)
    def _():
        total[...] += part
        middle_sum[...] += low

    @pl.when(h == pl.num_programs(0) - 1)
    def _():
        mid = middle_sum[...].astype(jnp.bfloat16)
        middle[0] = mid
        dh = (total[...] + dot(mid, factor_a[...], NT)) * gain[...]
        scaled = rows_in[0].astype(jnp.float32) * reciprocal[0]
        mean = jnp.mean(dh * scaled, axis=1, keepdims=True)
        change = reciprocal[0] * (dh - scaled * mean)
        share = change.shape[1] // len(order)
        for k, i in enumerate(order):
            here = slice(i * share, (i + 1) * share)
            result = upstream[:, here].astype(jnp.float32) + change[:, k * share : (k + 1) * share]
            input_gradient[:, here] = result.astype(jnp.bfloat16)


def backward(
    order,
    micro,
    rotated,
    upstream,
    keys,
    values,
    bias,
    cosine,
    sine,
    weight,
    factor_bt,
    factor_a,
    rows_in,
    reciprocal,
    gain,
    kept,
):
    micros, tokens, features = rotated.shape
    width = weight.shape[0]
    rank = factor_a.shape[1]
    ctx = keys.shape[0]
    block = features // KV_HEADS
    whole = lambda *dims: pl.BlockSpec(dims, lambda h, m: (0,) * len(dims))
    of_micro = lambda *dims: pl.BlockSpec(
        (1, *dims), lambda h, m: (m[0],) + (0,) * len(dims)
    )
    return pl.pallas_call(
        functools.partial(backward_kernel, order),
        grid_spec=pltpu.PrefetchScalarGridSpec(
            num_scalar_prefetch=1,
            grid=(KV_HEADS,),
            in_specs=[
                pl.BlockSpec((1, tokens, block), lambda h, m: (m[0], 0, h)),
                whole(tokens, features),
                pl.BlockSpec((ctx, HEAD_DIM), lambda h, m: (0, h)),
                pl.BlockSpec((ctx, HEAD_DIM), lambda h, m: (0, h)),
                of_micro(tokens, ctx),
                of_micro(tokens, HEAD_DIM),
                of_micro(tokens, HEAD_DIM),
                pl.BlockSpec((width, block), lambda h, m: (0, h)),
                pl.BlockSpec((block, rank), lambda h, m: (h, 0)),
                whole(width, rank),
                of_micro(tokens, width),
                of_micro(tokens, 1),
                whole(1, width),
            ]
            + [pl.BlockSpec(memory_space=pl.ANY)] * len(kept),
            out_specs=[
                whole(tokens, width),
                pl.BlockSpec((1, tokens, block), lambda h, m: (m[0], 0, h)),
                of_micro(tokens, rank),
            ],
            scratch_shapes=[
                pltpu.VMEM((tokens, width), jnp.float32),
                pltpu.VMEM((tokens, rank), jnp.float32),
            ],
        ),
        out_shape=[
            jax.ShapeDtypeStruct((tokens, width), jnp.bfloat16),
            jax.ShapeDtypeStruct((micros, tokens, features), jnp.bfloat16),
            jax.ShapeDtypeStruct((micros, tokens, rank), jnp.bfloat16),
        ],
        input_output_aliases={14: 1, 15: 2} if kept else {},
        cost_estimate=pl.CostEstimate(
            flops=2 * tokens * features * (width + 3 * ctx),
            bytes_accessed=2 * width * features,
            transcendentals=tokens * HEADS * ctx,
        ),
        name="backward",
    )(
        micro,
        rotated,
        upstream,
        keys,
        values,
        bias,
        cosine,
        sine,
        weight,
        factor_bt,
        factor_a,
        rows_in,
        reciprocal,
        gain,
        *kept,
    )


def gather_small(adapter_a, adapter_bt, norm_gain):
    count = lax.axis_size("dp")
    packed = jnp.concatenate([adapter_a, adapter_bt, norm_gain[:, None]], axis=1)
    sent = jnp.broadcast_to(packed[None], (count, *packed.shape))
    return lax.all_to_all(sent, "dp", split_axis=0, concat_axis=0, tiled=True)


def summed_shares(grad_a, grad_bt, order):
    count = lax.axis_size("dp")
    width, rank = grad_a.shape
    share = width // count
    walked = grad_a.reshape(count, share, rank)
    grad_a = jnp.concatenate([walked[order.index(i)][None] for i in range(count)], axis=0)
    both = jnp.concatenate([grad_a, grad_bt.reshape(count, share, rank)], axis=2)
    packed = jnp.concatenate([both[:, : share // 2], both[:, share // 2 :]], axis=2)
    got = lax.all_to_all(packed, "dp", split_axis=0, concat_axis=0, tiled=True)
    total = jnp.sum(got, axis=0)
    total = jnp.concatenate([total[:, : 2 * rank], total[:, 2 * rank :]], axis=0)
    return total[:, :rank], total[:, rank:]


def per_device(
    layer_inputs,
    top_grad,
    keys,
    values,
    query_weight,
    adapter_a,
    adapter_bt,
    norm_gain,
    offsets,
    segments,
):
    order = ring_order(lax.axis_size("dp"))
    _, _, micros, tokens, width = layer_inputs.shape
    rows = micros * tokens
    ctx = keys.shape[2]
    keys, values = keys[0, 0], values[0, 0]
    features = query_weight.shape[2]
    rank = adapter_a.shape[2]

    weight = lax.all_gather(
        query_weight[0], "dp", axis=0, tiled=True, axis_index_groups=[order]
    )
    small = gather_small(adapter_a[0], adapter_bt[0], norm_gain[0])
    factor_bt = small[:, :, rank : 2 * rank].reshape(features, rank)
    walked = jnp.concatenate([small[i : i + 1] for i in order], axis=0)
    factor_a = walked[:, :, :rank].reshape(width, rank)
    gain = walked[:, :, 2 * rank].reshape(1, width).astype(jnp.float32)

    rows_in = reordered(layer_inputs[0, 0], order)
    flat = rows_in.reshape(rows, width).astype(jnp.float32)
    reciprocal = lax.rsqrt(jnp.mean(flat * flat, axis=1, keepdims=True) + norm_eps)
    normed = (flat * reciprocal * gain).astype(jnp.bfloat16)
    lowrank = dot(normed, factor_a).astype(jnp.bfloat16)

    positions = (
        offsets[0][:, None] + jnp.arange(tokens, dtype=jnp.int32)[None, :]
    ).reshape(rows)
    seg_row = segments[0]
    place = jnp.arange(ctx, dtype=jnp.int32)
    query_seg = jnp.take(seg_row, positions)
    visible = (place[None, :] <= positions[:, None]) & (
        (seg_row[None, :] == 0) | (seg_row[None, :] == query_seg[:, None])
    )
    bias = jnp.where(visible, 0.0, -1e30).astype(jnp.float32)
    cosine, sine = rope_tables(positions)

    rotated = project(normed, lowrank, weight, factor_bt, cosine, sine)

    by_micro = lambda a: a.reshape(micros, tokens, a.shape[-1])
    section_count = lax.axis_size("pipe")
    section = lax.axis_index("pipe")
    last = section_count - 1
    steps = 2 * last + micros
    kept, results, arrived = (), [], []
    for step in range(steps):
        micro = jnp.clip(step - 2 * (last - section), 0, micros - 1)
        upstream = top_grad[0, min(step, micros - 1)]
        if step >= 2:
            upstream = jnp.where(section == last, upstream, arrived[step - 2])
        result, *kept = backward(
            order,
            micro.reshape(1).astype(jnp.int32),
            by_micro(rotated),
            upstream,
            keys,
            values,
            by_micro(bias),
            by_micro(cosine),
            by_micro(sine),
            weight,
            factor_bt,
            factor_a,
            rows_in,
            by_micro(reciprocal),
            gain,
            kept,
        )
        results.append(result)
        if step < steps - 2:
            arrived.append(
                lax.ppermute(result, "pipe", [(s, s - 1) for s in range(1, section_count)])
            )

    def of_micro(m):
        chosen = results[m]
        for back in range(1, section_count):
            chosen = jnp.where(last - section == back, results[m + 2 * back], chosen)
        return chosen

    grads = jnp.stack([of_micro(m) for m in range(micros)])
    dquery = kept[0].reshape(rows, features)
    middle = kept[1].reshape(rows, -1)
    share_a, share_bt = summed_shares(
        dot(normed, middle, TN), dot(dquery, lowrank, TN), order
    )
    return (grads[None, None], share_a[None], share_bt[None])


def solution(mesh):
    placed = (
        P("pipe", "dp", None, None, None),
        P("dp", None, None, None),
        P("pipe", "dp", None, None),
        P("pipe", "dp", None, None),
        P("pipe", "dp", None),
        P("pipe", "dp", None),
        P("pipe", "dp", None),
        P("pipe", "dp"),
        P("dp", None),
        P("dp", None),
    )
    return jax.shard_map(
        per_device,
        mesh=mesh,
        in_specs=placed,
        out_specs=(
            P("pipe", "dp", None, None, None),
            P("pipe", "dp", None),
            P("pipe", "dp", None),
        ),
        check_vma=False,
    )
```

```python
import functools

import jax
import jax.numpy as jnp
from jax import lax
from jax.experimental import pallas as pl
from jax.experimental.pallas import tpu as pltpu
from jax.sharding import PartitionSpec as P

HEADS = 20
KV_HEADS = 4
HEAD_DIM = 128
GROUP = HEADS // KV_HEADS
CHUNK = 16

norm_eps = 1e-06
rope_base = 1000000.0
SCALE = 1.0 / HEAD_DIM**0.5

NT = (((1,), (1,)), ((), ()))
TN = (((0,), (0,)), ((), ()))


def dot(a, b, dims=(((1,), (0,)), ((), ()))):
    return lax.dot_general(a, b, dims, preferred_element_type=jnp.float32)


def rope_tables(positions):
    half = HEAD_DIM // 2
    expon = jnp.arange(half, dtype=jnp.float32) * (2.0 / HEAD_DIM)
    inverse = rope_base ** (-expon)
    angles = positions.astype(jnp.float32)[:, None] * inverse[None, :]
    cosine, sine = jnp.cos(angles), jnp.sin(angles)
    return (
        jnp.concatenate([cosine, cosine], axis=1),
        jnp.concatenate([-sine, sine], axis=1),
    )


def ring_order(count):
    if count % 4:
        return list(range(count))
    chips = count // 2
    columns = 2 ** ((chips.bit_length() - 1) // 2)
    lines = chips // columns
    walk = [(z, 0) for z in range(lines)]
    for step, z in enumerate(range(lines - 1, -1, -1)):
        side = range(1, columns) if step % 2 == 0 else range(columns - 1, 0, -1)
        walk += [(z, x) for x in side]
    return [(z * columns + x) * 2 + core for z, x in walk for core in range(2)]


def reordered(value, order):
    share = value.shape[-1] // len(order)
    return jnp.concatenate(
        [value[..., i * share : (i + 1) * share] for i in order], axis=-1
    )


def in_hbm(value):
    return pltpu.with_memory_space_constraint(value, pltpu.HBM)


def stacked(value):
    return jnp.concatenate(
        [value[:, j * HEAD_DIM : (j + 1) * HEAD_DIM] for j in range(GROUP)], axis=0
    )


def step_kernel(order, step, chosen, *refs):
    refs = list(refs)
    first = step == 0
    own = refs.pop(0)
    incoming = refs.pop(0) if step >= 2 else None
    normed, lowrank = (refs.pop(0), refs.pop(0)) if first else (None, None)
    rotated = None if first else refs.pop(0)
    keys, values, bias, cosine, sine, weight, factor_bt, factor_a = refs[:8]
    rows_in, reciprocal, gain = refs[8:11]
    if first:
        held, rotated, input_gradient, dquery, middle, grads = refs[11:17]
        sems = refs[-1]
        upstream, dq, total, middle_sum = refs[-5:-1]
    else:
        held = weight
        input_gradient, dquery, middle, grads = refs[-9:-5]
        upstream, dq, total, middle_sum = refs[-4:]
    h = pl.program_id(0)
    groups = pl.num_programs(0) - 1
    micro = chosen[step]
    tokens = bias.shape[1]
    width = gain.shape[1]
    block = GROUP * HEAD_DIM
    columns = lambda g: pl.ds(pl.multiple_of(g * block, HEAD_DIM), block)
    fetch = lambda g: pltpu.make_async_copy(
        weight.at[:, columns(g)], held.at[g], sems.at[g]
    )

    @pl.when(h == 0)
    def _():
        if first:
            fetch(0).start()
            fetch(1).start()
        total[...] = jnp.zeros_like(total)
        middle_sum[...] = jnp.zeros_like(middle_sum)
        if incoming is None:
            upstream[...] = own[0]
        else:
            is_last = chosen[chosen.shape[0] - 1] == 1
            upstream[...] = jnp.where(is_last, own[0], incoming[...])

    def project():
        query = dot(normed[...], held[h]) + dot(lowrank[...], factor_bt[columns(h), :], NT)
        for m in range(rotated.shape[0] // tokens):
            rows = slice(m * tokens, (m + 1) * tokens)
            for j in range(GROUP):
                part = query[rows, j * HEAD_DIM : (j + 1) * HEAD_DIM]
                turned = part * cosine[m] + pltpu.roll(part, HEAD_DIM // 2, 1) * sine[m]
                rotated[rows, j * HEAD_DIM : (j + 1) * HEAD_DIM] = turned.astype(jnp.bfloat16)

    def pull_back(piece, before):
        at = slice(piece * (width // GROUP), (piece + 1) * (width // GROUP))
        total[:, at] += dot(before, held[h - 1, at, :], NT)

    def attend(before=None):
        if first:
            mine = rotated[pl.ds(pl.multiple_of(micro * tokens, tokens), tokens), :]
        else:
            mine = rotated[...]
        scores = dot(stacked(mine), keys[...], NT)
        dprobs = dot(stacked(upstream[:, columns(h)]), values[...], NT)
        dscores = []
        for j in range(GROUP):
            for row in range(0, tokens, CHUNK):
                at = slice(j * tokens + row, j * tokens + row + CHUNK)
                masked = scores[at] * SCALE + bias[0, row : row + CHUNK]
                expo = jnp.exp(masked - jnp.max(masked, axis=-1, keepdims=True))
                probs = expo * (1.0 / jnp.sum(expo, axis=-1, keepdims=True))
                rounded = probs.astype(jnp.bfloat16).astype(jnp.float32)
                delta = jnp.sum(rounded * dprobs[at], axis=-1, keepdims=True)
                dscores.append((probs * (dprobs[at] - delta) * SCALE).astype(jnp.bfloat16))
            if before is not None:
                pull_back(j, before)
        drot = dot(jnp.concatenate(dscores, axis=0), keys[...])
        for j in range(GROUP):
            part = drot[j * tokens : (j + 1) * tokens]
            turned = part * cosine[micro] - pltpu.roll(part, HEAD_DIM // 2, 1) * sine[micro]
            at = slice(j * HEAD_DIM, (j + 1) * HEAD_DIM)
            dq[:, at] = turned.astype(jnp.bfloat16)
            dquery[0, :, at] = turned.astype(jnp.bfloat16)
        middle_sum[...] += dot(dq[...], factor_bt[columns(h), :])

    @pl.when(h == 0)
    def _():
        if first:
            fetch(h).wait()
            project()
        attend()

    if first:

        @pl.when((h > 0) & (h + 1 < groups))
        def _():
            fetch(h + 1).start()

    @pl.when((h > 0) & (h < groups))
    def _():
        if first:
            fetch(h).wait()
            project()
        attend(dq[...])

    @pl.when(h == groups)
    def _():
        for piece in range(GROUP):
            pull_back(piece, dq[...])
        mid = middle_sum[...].astype(jnp.bfloat16)
        middle[0] = mid
        dh = (total[...] + dot(mid, factor_a[...], NT)) * gain[...]
        scaled = rows_in[0].astype(jnp.float32) * reciprocal[0]
        mean = jnp.mean(dh * scaled, axis=1, keepdims=True)
        change = reciprocal[0] * (dh - scaled * mean)
        share = change.shape[1] // len(order)
        for k, i in enumerate(order):
            here = slice(i * share, (i + 1) * share)
            result = upstream[:, here].astype(jnp.float32) + change[:, k * share : (k + 1) * share]
            input_gradient[:, here] = result.astype(jnp.bfloat16)
        grads[0] = input_gradient[...]


def backward(
    order,
    step,
    chosen,
    own,
    incoming,
    normed,
    lowrank,
    rotated,
    keys,
    values,
    bias,
    cosine,
    sine,
    weight,
    factor_bt,
    factor_a,
    rows_in,
    reciprocal,
    gain,
    kept,
):
    first = step == 0
    micros, tokens, features = own.shape
    width, rank = factor_a.shape
    ctx = keys.shape[0]
    rows = micros * tokens
    block = features // KV_HEADS
    group = lambda h: jnp.minimum(h, KV_HEADS - 1)
    whole = lambda *dims: pl.BlockSpec(dims, lambda h, m: (0,) * len(dims))
    of_micro = lambda *dims: pl.BlockSpec(
        (1, *dims), lambda h, m: (m[step],) + (0,) * len(dims)
    )
    untouched = pl.BlockSpec(memory_space=pl.ANY)
    of_group = lambda dim: pl.BlockSpec((dim, HEAD_DIM), lambda h, m: (0, group(h)))
    ins = [(own, of_micro(tokens, features))]
    if first:
        ins += [(normed, whole(rows, width)), (lowrank, whole(rows, rank))]
    else:
        if incoming is not None:
            ins.append((incoming, whole(tokens, features)))
        ins += [
            (rotated, pl.BlockSpec((tokens, block), lambda h, m: (m[step], group(h)))),
        ]
    ins += [
        (keys, of_group(ctx)),
        (values, of_group(ctx)),
        (bias, of_micro(tokens, ctx)),
        (cosine, whole(micros, tokens, HEAD_DIM)),
        (sine, whole(micros, tokens, HEAD_DIM)),
        (weight, untouched if first else pl.BlockSpec(memory_space=pltpu.VMEM)),
        (factor_bt, whole(features, rank)),
        (factor_a, whole(width, rank)),
        (rows_in, of_micro(tokens, width)),
        (reciprocal, of_micro(tokens, 1)),
        (gain, whole(1, width)),
    ]
    ins += [(a, untouched) for a in kept]
    outs = [
        (pltpu.HBM((tokens, width), jnp.bfloat16), whole(tokens, width)),
        (
            pltpu.HBM((micros, tokens, features), jnp.bfloat16),
            pl.BlockSpec((1, tokens, block), lambda h, m: (m[step], 0, group(h))),
        ),
        (pltpu.HBM((micros, tokens, rank), jnp.bfloat16), of_micro(tokens, rank)),
        (pltpu.HBM((micros, tokens, width), jnp.bfloat16), of_micro(tokens, width)),
    ]
    scratch = [
        pltpu.VMEM((tokens, features), jnp.bfloat16),
        pltpu.VMEM((tokens, block), jnp.bfloat16),
        pltpu.VMEM((tokens, width), jnp.float32),
        pltpu.VMEM((tokens, rank), jnp.float32),
    ]
    if first:
        outs[:0] = [
            (
                pltpu.VMEM((KV_HEADS, width, block), jnp.bfloat16),
                pl.BlockSpec(memory_space=pltpu.VMEM),
            ),
            (
                pltpu.HBM((rows, features), jnp.bfloat16),
                pl.BlockSpec((rows, block), lambda h, m: (0, group(h))),
            ),
        ]
        scratch.append(pltpu.SemaphoreType.DMA((KV_HEADS,)))
        aliases = {}
    else:
        outs.append(
            (
                pltpu.VMEM((KV_HEADS, width, block), jnp.bfloat16),
                pl.BlockSpec(memory_space=pltpu.VMEM),
            )
        )
        at = [a is weight for a, _ in ins].index(True)
        aliases = {1 + at: 4, len(ins) - 2: 1, len(ins) - 1: 2, len(ins): 3}
    return pl.pallas_call(
        functools.partial(step_kernel, order, step),
        grid_spec=pltpu.PrefetchScalarGridSpec(
            num_scalar_prefetch=1,
            grid=(KV_HEADS + 1,),
            in_specs=[spec for _, spec in ins],
            out_specs=[spec for _, spec in outs],
            scratch_shapes=scratch,
        ),
        out_shape=[shape for shape, _ in outs],
        input_output_aliases=aliases,
        compiler_params=pltpu.CompilerParams(vmem_limit_bytes=24 * 2**20),
        cost_estimate=pl.CostEstimate(
            flops=2 * tokens * features * (width + 3 * ctx),
            bytes_accessed=2 * width * features,
            transcendentals=tokens * HEADS * ctx,
        ),
        name="first_step" if first else "step",
    )(chosen, *(a if a is incoming or (a is weight and not first) else in_hbm(a) for a, _ in ins))


def gradients_kernel(order, normed, middle, dquery, lowrank, out):
    of_a = dot(middle[...], normed[...], TN)
    of_bt = dot(lowrank[...], dquery[...], TN)
    rank = of_a.shape[0]
    share = out.shape[2]
    for k, i in enumerate(order):
        out[i, :rank] = of_a[:, k * share : (k + 1) * share].astype(out.dtype)
        out[k, rank:] = of_bt[:, k * share : (k + 1) * share].astype(out.dtype)


def gradients(order, normed, middle, dquery, lowrank):
    rows, width = normed.shape
    rank = middle.shape[1]
    count = len(order)
    return pl.pallas_call(
        functools.partial(gradients_kernel, order),
        out_shape=jax.ShapeDtypeStruct((count, 2 * rank, width // count), jnp.float32),
        name="gradients",
    )(normed, middle, dquery, lowrank)


def gather_small(adapter_a, adapter_bt, norm_gain):
    count = lax.axis_size("dp")
    packed = jnp.concatenate([adapter_a, adapter_bt, norm_gain[:, None]], axis=1)
    sent = jnp.broadcast_to(packed[None], (count, *packed.shape))
    return lax.all_to_all(sent, "dp", split_axis=0, concat_axis=0, tiled=True)


def per_device(
    layer_inputs,
    top_grad,
    keys,
    values,
    query_weight,
    adapter_a,
    adapter_bt,
    norm_gain,
    offsets,
    segments,
):
    order = ring_order(lax.axis_size("dp"))
    _, _, micros, tokens, width = layer_inputs.shape
    rows = micros * tokens
    ctx = keys.shape[2]
    keys, values = keys[0, 0], values[0, 0]
    features = query_weight.shape[2]
    rank = adapter_a.shape[2]

    weight = lax.all_gather(
        query_weight[0], "dp", axis=0, tiled=True, axis_index_groups=[order]
    )
    small = gather_small(adapter_a[0], adapter_bt[0], norm_gain[0])
    factor_bt = small[:, :, rank : 2 * rank].reshape(features, rank)
    walked = jnp.concatenate([small[i : i + 1] for i in order], axis=0)
    factor_a = walked[:, :, :rank].reshape(width, rank)
    gain = walked[:, :, 2 * rank].reshape(1, width).astype(jnp.float32)

    rows_in = reordered(layer_inputs[0, 0], order)
    flat = rows_in.reshape(rows, width).astype(jnp.float32)
    reciprocal = lax.rsqrt(jnp.mean(flat * flat, axis=1, keepdims=True) + norm_eps)
    normed = (flat * reciprocal * gain).astype(jnp.bfloat16)
    lowrank = dot(normed, factor_a).astype(jnp.bfloat16)

    positions = (
        offsets[0][:, None] + jnp.arange(tokens, dtype=jnp.int32)[None, :]
    ).reshape(rows)
    seg_row = segments[0]
    place = jnp.arange(ctx, dtype=jnp.int32)
    query_seg = jnp.take(seg_row, positions)
    visible = (place[None, :] <= positions[:, None]) & (
        (seg_row[None, :] == 0) | (seg_row[None, :] == query_seg[:, None])
    )
    bias = jnp.where(visible, 0.0, -1e30).astype(jnp.float32)
    cosine, sine = rope_tables(positions)

    by_micro = lambda a: a.reshape(micros, tokens, a.shape[-1])
    section_count = lax.axis_size("pipe")
    section = lax.axis_index("pipe")
    last = section_count - 1
    steps = 2 * last + micros
    kept, arrived, rotated = (), [], None
    micro = jnp.clip(jnp.arange(steps) - 2 * (last - section), 0, micros - 1)
    chosen = jnp.append(micro, section == last).astype(jnp.int32)
    bias, cosine, sine, reciprocal = map(by_micro, (bias, cosine, sine, reciprocal))
    for step in range(steps):
        made = list(
            backward(
                order,
                step,
                chosen,
                top_grad[0],
                arrived[step - 2] if step >= 2 else None,
                normed,
                lowrank,
                rotated,
                keys,
                values,
                bias,
                cosine,
                sine,
                weight,
                factor_bt,
                factor_a,
                rows_in,
                reciprocal,
                gain,
                kept,
            )
        )
        if rotated is None:
            weight, rotated = made.pop(0), made.pop(0)
        else:
            weight = made.pop()
        result, *kept = made
        if step < steps - 2:
            arrived.append(
                lax.ppermute(result, "pipe", [(s, s - 1) for s in range(1, section_count)])
            )

    grads = kept[2]
    dquery = kept[0].reshape(rows, features)
    middle = kept[1].reshape(rows, -1)
    partial = gradients(order, normed, middle, dquery, lowrank)
    got = lax.all_to_all(partial, "dp", split_axis=0, concat_axis=0, tiled=True)
    total = jnp.sum(got.astype(jnp.float32), axis=0)
    return (grads[None, None], total[:rank].T[None], total[rank:].T[None])


def solution(mesh):
    placed = (
        P("pipe", "dp", None, None, None),
        P("dp", None, None, None),
        P("pipe", "dp", None, None),
        P("pipe", "dp", None, None),
        P("pipe", "dp", None),
        P("pipe", "dp", None),
        P("pipe", "dp", None),
        P("pipe", "dp"),
        P("dp", None),
        P("dp", None),
    )
    return jax.shard_map(
        per_device,
        mesh=mesh,
        in_specs=placed,
        out_specs=(
            P("pipe", "dp", None, None, None),
            P("pipe", "dp", None),
            P("pipe", "dp", None),
        ),
        check_vma=False,
    )
```

```python
import functools

import jax
import jax.numpy as jnp
from jax import lax
from jax.experimental import pallas as pl
from jax.experimental.pallas import tpu as pltpu
from jax.sharding import PartitionSpec as P

HEADS = 20
KV_HEADS = 4
HEAD_DIM = 128
GROUP = HEADS // KV_HEADS
CHUNK = 16

norm_eps = 1e-06
rope_base = 1000000.0
SCALE = 1.0 / HEAD_DIM**0.5

NT = (((1,), (1,)), ((), ()))
TN = (((0,), (0,)), ((), ()))


def dot(a, b, dims=(((1,), (0,)), ((), ()))):
    return lax.dot_general(a, b, dims, preferred_element_type=jnp.float32)


def rope_tables(positions):
    half = HEAD_DIM // 2
    expon = jnp.arange(half, dtype=jnp.float32) * (2.0 / HEAD_DIM)
    inverse = rope_base ** (-expon)
    angles = positions.astype(jnp.float32)[:, None] * inverse[None, :]
    cosine, sine = jnp.cos(angles), jnp.sin(angles)
    return (
        jnp.concatenate([cosine, cosine], axis=1),
        jnp.concatenate([-sine, sine], axis=1),
    )


def ring_order(count):
    if count % 4:
        return list(range(count))
    chips = count // 2
    columns = 2 ** ((chips.bit_length() - 1) // 2)
    lines = chips // columns
    walk = [(z, 0) for z in range(lines)]
    for step, z in enumerate(range(lines - 1, -1, -1)):
        side = range(1, columns) if step % 2 == 0 else range(columns - 1, 0, -1)
        walk += [(z, x) for x in side]
    return [(z * columns + x) * 2 + core for z, x in walk for core in range(2)]


def reordered(value, order):
    share = value.shape[-1] // len(order)
    return jnp.concatenate(
        [value[..., i * share : (i + 1) * share] for i in order], axis=-1
    )


def in_hbm(value):
    return pltpu.with_memory_space_constraint(value, pltpu.HBM)


def stacked(value):
    return jnp.concatenate(
        [value[:, j * HEAD_DIM : (j + 1) * HEAD_DIM] for j in range(GROUP)], axis=0
    )


def step_kernel(order, step, chosen, *refs):
    refs = list(refs)
    first = step == 0
    own = refs.pop(0)
    incoming = refs.pop(0) if step >= 2 else None
    normed, lowrank = (refs.pop(0), refs.pop(0)) if first else (None, None)
    rotated = None if first else refs.pop(0)
    keys, values, bias, cosine, sine, weight, factor_bt, factor_a = refs[:8]
    rows_in, reciprocal, gain = refs[8:11]
    if first:
        held, rotated, input_gradient, dquery, middle, grads = refs[11:17]
        sems = refs[-1]
        upstream, dq, total, middle_sum = refs[-5:-1]
    else:
        held = weight
        input_gradient, dquery, middle, grads = refs[-9:-5]
        upstream, dq, total, middle_sum = refs[-4:]
    h = pl.program_id(0)
    groups = pl.num_programs(0) - 1
    micro = chosen[step]
    tokens = bias.shape[1]
    width = gain.shape[1]
    block = GROUP * HEAD_DIM
    columns = lambda g: pl.ds(pl.multiple_of(g * block, HEAD_DIM), block)
    fetch = lambda g: pltpu.make_async_copy(
        weight.at[:, columns(g)], held.at[g], sems.at[g]
    )

    @pl.when(h == 0)
    def _():
        if first:
            fetch(0).start()
            fetch(1).start()
        total[...] = jnp.zeros_like(total)
        middle_sum[...] = jnp.zeros_like(middle_sum)
        if incoming is None:
            upstream[...] = own[0]
        else:
            is_last = chosen[chosen.shape[0] - 1] == 1
            upstream[...] = jnp.where(is_last, own[0], incoming[...])

    def project():
        query = dot(normed[...], held[h]) + dot(lowrank[...], factor_bt[columns(h), :], NT)
        for m in range(rotated.shape[0] // tokens):
            rows = slice(m * tokens, (m + 1) * tokens)
            for j in range(GROUP):
                part = query[rows, j * HEAD_DIM : (j + 1) * HEAD_DIM]
                turned = part * cosine[m] + pltpu.roll(part, HEAD_DIM // 2, 1) * sine[m]
                rotated[rows, j * HEAD_DIM : (j + 1) * HEAD_DIM] = turned.astype(jnp.bfloat16)

    def pull_back(piece, before):
        at = slice(piece * (width // GROUP), (piece + 1) * (width // GROUP))
        total[:, at] += dot(before, held[h - 1, at, :], NT)

    def attend(before=None):
        if first:
            mine = rotated[pl.ds(pl.multiple_of(micro * tokens, tokens), tokens), :]
        else:
            mine = rotated[...]
        scores = dot(stacked(mine), keys[...], NT)
        dprobs = dot(stacked(upstream[:, columns(h)]), values[...], NT)
        dscores = []
        for j in range(GROUP):
            for row in range(0, tokens, CHUNK):
                at = slice(j * tokens + row, j * tokens + row + CHUNK)
                masked = scores[at] * SCALE + bias[0, row : row + CHUNK]
                expo = jnp.exp(masked - jnp.max(masked, axis=-1, keepdims=True))
                probs = expo * (1.0 / jnp.sum(expo, axis=-1, keepdims=True))
                rounded = probs.astype(jnp.bfloat16).astype(jnp.float32)
                delta = jnp.sum(rounded * dprobs[at], axis=-1, keepdims=True)
                dscores.append((probs * (dprobs[at] - delta) * SCALE).astype(jnp.bfloat16))
            if before is not None:
                pull_back(j, before)
        drot = dot(jnp.concatenate(dscores, axis=0), keys[...])
        for j in range(GROUP):
            part = drot[j * tokens : (j + 1) * tokens]
            turned = part * cosine[micro] - pltpu.roll(part, HEAD_DIM // 2, 1) * sine[micro]
            at = slice(j * HEAD_DIM, (j + 1) * HEAD_DIM)
            dq[:, at] = turned.astype(jnp.bfloat16)
            dquery[0, :, at] = turned.astype(jnp.bfloat16)
        middle_sum[...] += dot(dq[...], factor_bt[columns(h), :])

    @pl.when(h == 0)
    def _():
        if first:
            fetch(h).wait()
            project()
        attend()

    if first:

        @pl.when((h > 0) & (h + 1 < groups))
        def _():
            fetch(h + 1).start()

    @pl.when((h > 0) & (h < groups))
    def _():
        if first:
            fetch(h).wait()
            project()
        attend(dq[...])

    @pl.when(h == groups)
    def _():
        for piece in range(GROUP):
            pull_back(piece, dq[...])
        mid = middle_sum[...].astype(jnp.bfloat16)
        middle[0] = mid
        dh = (total[...] + dot(mid, factor_a[...], NT)) * gain[...]
        scaled = rows_in[0].astype(jnp.float32) * reciprocal[0]
        mean = jnp.mean(dh * scaled, axis=1, keepdims=True)
        change = reciprocal[0] * (dh - scaled * mean)
        share = change.shape[1] // len(order)
        for k, i in enumerate(order):
            here = slice(i * share, (i + 1) * share)
            result = upstream[:, here].astype(jnp.float32) + change[:, k * share : (k + 1) * share]
            input_gradient[:, here] = result.astype(jnp.bfloat16)
        grads[0] = input_gradient[...]


def backward(
    order,
    step,
    chosen,
    own,
    incoming,
    normed,
    lowrank,
    rotated,
    keys,
    values,
    bias,
    cosine,
    sine,
    weight,
    factor_bt,
    factor_a,
    rows_in,
    reciprocal,
    gain,
    kept,
):
    first = step == 0
    micros, tokens, features = own.shape
    width, rank = factor_a.shape
    ctx = keys.shape[0]
    rows = micros * tokens
    block = features // KV_HEADS
    group = lambda h: jnp.minimum(h, KV_HEADS - 1)
    whole = lambda *dims: pl.BlockSpec(dims, lambda h, m: (0,) * len(dims))
    of_micro = lambda *dims: pl.BlockSpec(
        (1, *dims), lambda h, m: (m[step],) + (0,) * len(dims)
    )
    untouched = pl.BlockSpec(memory_space=pl.ANY)
    of_group = lambda dim: pl.BlockSpec((dim, HEAD_DIM), lambda h, m: (0, group(h)))
    ins = [(own, of_micro(tokens, features))]
    if first:
        ins += [(normed, whole(rows, width)), (lowrank, whole(rows, rank))]
    else:
        if incoming is not None:
            ins.append((incoming, whole(tokens, features)))
        ins += [
            (rotated, pl.BlockSpec((tokens, block), lambda h, m: (m[step], group(h)))),
        ]
    ins += [
        (keys, of_group(ctx)),
        (values, of_group(ctx)),
        (bias, of_micro(tokens, ctx)),
        (cosine, whole(micros, tokens, HEAD_DIM)),
        (sine, whole(micros, tokens, HEAD_DIM)),
        (weight, untouched if first else pl.BlockSpec(memory_space=pltpu.VMEM)),
        (factor_bt, whole(features, rank)),
        (factor_a, whole(width, rank)),
        (rows_in, of_micro(tokens, width)),
        (reciprocal, of_micro(tokens, 1)),
        (gain, whole(1, width)),
    ]
    ins += [(a, untouched) for a in kept]
    outs = [
        (pltpu.HBM((tokens, width), jnp.bfloat16), whole(tokens, width)),
        (
            pltpu.HBM((micros, tokens, features), jnp.bfloat16),
            pl.BlockSpec((1, tokens, block), lambda h, m: (m[step], 0, group(h))),
        ),
        (pltpu.HBM((micros, tokens, rank), jnp.bfloat16), of_micro(tokens, rank)),
        (pltpu.HBM((micros, tokens, width), jnp.bfloat16), of_micro(tokens, width)),
    ]
    scratch = [
        pltpu.VMEM((tokens, features), jnp.bfloat16),
        pltpu.VMEM((tokens, block), jnp.bfloat16),
        pltpu.VMEM((tokens, width), jnp.float32),
        pltpu.VMEM((tokens, rank), jnp.float32),
    ]
    if first:
        outs[:0] = [
            (
                pltpu.VMEM((KV_HEADS, width, block), jnp.bfloat16),
                pl.BlockSpec(memory_space=pltpu.VMEM),
            ),
            (
                pltpu.HBM((rows, features), jnp.bfloat16),
                pl.BlockSpec((rows, block), lambda h, m: (0, group(h))),
            ),
        ]
        scratch.append(pltpu.SemaphoreType.DMA((KV_HEADS,)))
        aliases = {}
    else:
        outs.append(
            (
                pltpu.VMEM((KV_HEADS, width, block), jnp.bfloat16),
                pl.BlockSpec(memory_space=pltpu.VMEM),
            )
        )
        at = [a is weight for a, _ in ins].index(True)
        aliases = {1 + at: 4, len(ins) - 2: 1, len(ins) - 1: 2, len(ins): 3}
    return pl.pallas_call(
        functools.partial(step_kernel, order, step),
        grid_spec=pltpu.PrefetchScalarGridSpec(
            num_scalar_prefetch=1,
            grid=(KV_HEADS + 1,),
            in_specs=[spec for _, spec in ins],
            out_specs=[spec for _, spec in outs],
            scratch_shapes=scratch,
        ),
        out_shape=[shape for shape, _ in outs],
        input_output_aliases=aliases,
        compiler_params=pltpu.CompilerParams(vmem_limit_bytes=24 * 2**20),
        cost_estimate=pl.CostEstimate(
            flops=2 * tokens * features * (width + 3 * ctx),
            bytes_accessed=2 * width * features,
            transcendentals=tokens * HEADS * ctx,
        ),
        name="first_step" if first else "step",
    )(chosen, *(a if a is incoming or (a is weight and not first) else in_hbm(a) for a, _ in ins))


def gradients_kernel(order, normed, middle, dquery, lowrank, out):
    of_a = dot(middle[...], normed[...], TN)
    of_bt = dot(lowrank[...], dquery[...], TN)
    rank = of_a.shape[0]
    share = of_a.shape[1] // len(order)
    lanes = out.shape[2]
    for k, i in enumerate(order):
        for to, top, value in ((i, 0, of_a), (k, rank, of_bt)):
            mine = value[:, k * share : (k + 1) * share].astype(out.dtype)
            if share <= lanes:
                out[to, top : top + rank, :] = mine
                continue
            out[to, top : top + rank, :] = mine[:, :lanes]
            over = share - lanes
            side = lanes // over
            deep = rank // side
            folded = [mine[n * deep : (n + 1) * deep, lanes:] for n in range(side)]
            low = 2 * rank + top // side
            out[to, low : low + deep, :] = jnp.concatenate(folded, axis=1)


def gradients(order, normed, middle, dquery, lowrank):
    rows, width = normed.shape
    rank = middle.shape[1]
    count = len(order)
    share = width // count
    lanes = min(share, HEAD_DIM)
    deep = 2 * rank * share // lanes
    return pl.pallas_call(
        functools.partial(gradients_kernel, order),
        out_shape=jax.ShapeDtypeStruct((count, deep, lanes), jnp.bfloat16),
        name="gradients",
    )(normed, middle, dquery, lowrank)


def unfolded(total, rank, share):
    lanes = total.shape[1]
    if share == lanes:
        return total
    over = share - lanes
    side = lanes // over
    deep = rank // side
    parts = []
    for top in (0, rank):
        low = 2 * rank + top // side
        folded = total[low : low + deep]
        parts.append(
            jnp.concatenate([folded[:, n * over : (n + 1) * over] for n in range(side)], axis=0)
        )
    return jnp.concatenate([total[: 2 * rank], jnp.concatenate(parts, axis=0)], axis=1)


def gather_small(adapter_a, adapter_bt, norm_gain):
    count = lax.axis_size("dp")
    packed = jnp.concatenate([adapter_a, adapter_bt, norm_gain[:, None]], axis=1)
    sent = jnp.broadcast_to(packed[None], (count, *packed.shape))
    return lax.all_to_all(sent, "dp", split_axis=0, concat_axis=0, tiled=True)


def per_device(
    layer_inputs,
    top_grad,
    keys,
    values,
    query_weight,
    adapter_a,
    adapter_bt,
    norm_gain,
    offsets,
    segments,
):
    order = ring_order(lax.axis_size("dp"))
    _, _, micros, tokens, width = layer_inputs.shape
    rows = micros * tokens
    ctx = keys.shape[2]
    keys, values = keys[0, 0], values[0, 0]
    features = query_weight.shape[2]
    rank = adapter_a.shape[2]

    weight = lax.all_gather(
        query_weight[0], "dp", axis=0, tiled=True, axis_index_groups=[order]
    )
    small = gather_small(adapter_a[0], adapter_bt[0], norm_gain[0])
    factor_bt = small[:, :, rank : 2 * rank].reshape(features, rank)
    walked = jnp.concatenate([small[i : i + 1] for i in order], axis=0)
    factor_a = walked[:, :, :rank].reshape(width, rank)
    gain = walked[:, :, 2 * rank].reshape(1, width).astype(jnp.float32)

    rows_in = reordered(layer_inputs[0, 0], order)
    flat = rows_in.reshape(rows, width).astype(jnp.float32)
    reciprocal = lax.rsqrt(jnp.mean(flat * flat, axis=1, keepdims=True) + norm_eps)
    normed = (flat * reciprocal * gain).astype(jnp.bfloat16)
    lowrank = dot(normed, factor_a).astype(jnp.bfloat16)

    positions = (
        offsets[0][:, None] + jnp.arange(tokens, dtype=jnp.int32)[None, :]
    ).reshape(rows)
    seg_row = segments[0]
    place = jnp.arange(ctx, dtype=jnp.int32)
    query_seg = jnp.take(seg_row, positions)
    visible = (place[None, :] <= positions[:, None]) & (
        (seg_row[None, :] == 0) | (seg_row[None, :] == query_seg[:, None])
    )
    bias = jnp.where(visible, 0.0, -1e30).astype(jnp.float32)
    cosine, sine = rope_tables(positions)

    by_micro = lambda a: a.reshape(micros, tokens, a.shape[-1])
    section_count = lax.axis_size("pipe")
    section = lax.axis_index("pipe")
    last = section_count - 1
    steps = 2 * last + micros
    kept, arrived, rotated = (), [], None
    micro = jnp.clip(jnp.arange(steps) - 2 * (last - section), 0, micros - 1)
    chosen = jnp.append(micro, section == last).astype(jnp.int32)
    bias, cosine, sine, reciprocal = map(by_micro, (bias, cosine, sine, reciprocal))
    for step in range(steps):
        made = list(
            backward(
                order,
                step,
                chosen,
                top_grad[0],
                arrived[step - 2] if step >= 2 else None,
                normed,
                lowrank,
                rotated,
                keys,
                values,
                bias,
                cosine,
                sine,
                weight,
                factor_bt,
                factor_a,
                rows_in,
                reciprocal,
                gain,
                kept,
            )
        )
        if rotated is None:
            weight, rotated = made.pop(0), made.pop(0)
        else:
            weight = made.pop()
        result, *kept = made
        if step < steps - 2:
            arrived.append(
                lax.ppermute(result, "pipe", [(s, s - 1) for s in range(1, section_count)])
            )

    grads = kept[2]
    dquery = kept[0].reshape(rows, features)
    middle = kept[1].reshape(rows, -1)
    partial = gradients(order, normed, middle, dquery, lowrank)
    got = lax.all_to_all(partial, "dp", split_axis=0, concat_axis=0, tiled=True)
    total = unfolded(jnp.sum(got.astype(jnp.float32), axis=0), rank, width // len(order))
    return (grads[None, None], total[:rank].T[None], total[rank:].T[None])


def solution(mesh):
    placed = (
        P("pipe", "dp", None, None, None),
        P("dp", None, None, None),
        P("pipe", "dp", None, None),
        P("pipe", "dp", None, None),
        P("pipe", "dp", None),
        P("pipe", "dp", None),
        P("pipe", "dp", None),
        P("pipe", "dp"),
        P("dp", None),
        P("dp", None),
    )
    return jax.shard_map(
        per_device,
        mesh=mesh,
        in_specs=placed,
        out_specs=(
            P("pipe", "dp", None, None, None),
            P("pipe", "dp", None),
            P("pipe", "dp", None),
        ),
        check_vma=False,
    )
```

```python
import functools

import jax
import jax.numpy as jnp
from jax import lax
from jax.experimental import pallas as pl
from jax.experimental.pallas import tpu as pltpu
from jax.sharding import PartitionSpec as P

HEADS = 20
KV_HEADS = 4
HEAD_DIM = 128
GROUP = HEADS // KV_HEADS
CHUNK = 16

norm_eps = 1e-06
rope_base = 1000000.0
SCALE = 1.0 / HEAD_DIM**0.5

NT = (((1,), (1,)), ((), ()))
TN = (((0,), (0,)), ((), ()))


def dot(a, b, dims=(((1,), (0,)), ((), ()))):
    return lax.dot_general(a, b, dims, preferred_element_type=jnp.float32)


def rope_tables(positions):
    half = HEAD_DIM // 2
    expon = jnp.arange(half, dtype=jnp.float32) * (2.0 / HEAD_DIM)
    inverse = rope_base ** (-expon)
    angles = positions.astype(jnp.float32)[:, None] * inverse[None, :]
    cosine, sine = jnp.cos(angles), jnp.sin(angles)
    return (
        jnp.concatenate([cosine, cosine], axis=1),
        jnp.concatenate([-sine, sine], axis=1),
    )


def ring_order(count):
    if count % 4:
        return list(range(count))
    chips = count // 2
    columns = 2 ** ((chips.bit_length() - 1) // 2)
    lines = chips // columns
    walk = [(z, 0) for z in range(lines)]
    for step, z in enumerate(range(lines - 1, -1, -1)):
        side = range(1, columns) if step % 2 == 0 else range(columns - 1, 0, -1)
        walk += [(z, x) for x in side]
    return [(z * columns + x) * 2 + core for z, x in walk for core in range(2)]


def reordered(value, order):
    share = value.shape[-1] // len(order)
    return jnp.concatenate(
        [value[..., i * share : (i + 1) * share] for i in order], axis=-1
    )


def stacked(value):
    return jnp.concatenate(
        [value[:, j * HEAD_DIM : (j + 1) * HEAD_DIM] for j in range(GROUP)], axis=0
    )


NEEDED_FIRST = (1, 2, 8, 6, 7)
NEEDED_NEXT = (0, 3, 4, 5)
NEEDED_LAST = (9, 10, 11, 12)


def in_hbm(value):
    return pltpu.with_memory_space_constraint(value, pltpu.HBM)


def step_kernel(order, step, chosen, *refs):
    first = step == 0
    refs = list(refs)
    given, weight = refs[:13], refs[13]
    arrays = given
    incoming = refs[14] if step >= 2 else None
    if first:
        held, rotated, input_gradient, dquery, middle, grads = refs[14:20]
        staged = refs[20:33]
        sems, stage_sems = refs[-2:]
        upstream, dq, total, middle_sum = refs[-6:-2]
        stage = lambda i: pltpu.make_async_copy(given[i], staged[i], stage_sems.at[i])
        arrays = staged
    else:
        held = weight
        rotated = refs[14 + (step >= 2)]
        input_gradient, dquery, middle, grads = refs[-9:-5]
        upstream, dq, total, middle_sum = refs[-4:]
    own, normed, lowrank, keys, values, bias, cosine, sine = arrays[:8]
    factor_bt, factor_a, rows_in, reciprocal, gain = arrays[8:]
    h = pl.program_id(0)
    groups = pl.num_programs(0) - 1
    micro = chosen[step]
    tokens = bias.shape[1]
    width = gain.shape[1]
    block = GROUP * HEAD_DIM
    columns = lambda g: pl.ds(pl.multiple_of(g * block, HEAD_DIM), block)
    fetch = lambda g: pltpu.make_async_copy(
        weight.at[:, columns(g)], held.at[g], sems.at[g]
    )

    @pl.when(h == 0)
    def _():
        if first:
            for i in NEEDED_FIRST:
                stage(i).start()
            fetch(0).start()
            for i in NEEDED_NEXT:
                stage(i).start()
            fetch(1).start()
            for i in NEEDED_LAST:
                stage(i).start()
            for i in NEEDED_FIRST:
                stage(i).wait()
        total[...] = jnp.zeros_like(total)
        middle_sum[...] = jnp.zeros_like(middle_sum)
        if first:
            pass
        elif incoming is None:
            upstream[...] = own[micro]
        else:
            is_last = chosen[chosen.shape[0] - 1] == 1
            upstream[...] = jnp.where(is_last, own[micro], incoming[...])

    def project():
        query = dot(normed[...], held[h]) + dot(lowrank[...], factor_bt[columns(h), :], NT)
        for m in range(rotated.shape[0] // tokens):
            rows = slice(m * tokens, (m + 1) * tokens)
            for j in range(GROUP):
                part = query[rows, j * HEAD_DIM : (j + 1) * HEAD_DIM]
                turned = part * cosine[m] + pltpu.roll(part, HEAD_DIM // 2, 1) * sine[m]
                at = pl.ds(pl.multiple_of(h * block + j * HEAD_DIM, HEAD_DIM), HEAD_DIM)
                rotated[rows, at] = turned.astype(jnp.bfloat16)

    def pull_back(piece, before):
        at = slice(piece * (width // GROUP), (piece + 1) * (width // GROUP))
        total[:, at] += dot(before, held[h - 1, at, :], NT)

    def attend(before=None):
        mine = rotated[pl.ds(pl.multiple_of(micro * tokens, tokens), tokens), columns(h)]
        head = pl.ds(pl.multiple_of(h * HEAD_DIM, HEAD_DIM), HEAD_DIM)
        scores = dot(stacked(mine), keys[:, head], NT)
        dprobs = dot(stacked(upstream[:, columns(h)]), values[:, head], NT)
        dscores = []
        for j in range(GROUP):
            for row in range(0, tokens, CHUNK):
                at = slice(j * tokens + row, j * tokens + row + CHUNK)
                masked = scores[at] * SCALE + bias[micro, row : row + CHUNK]
                expo = jnp.exp(masked - jnp.max(masked, axis=-1, keepdims=True))
                probs = expo * (1.0 / jnp.sum(expo, axis=-1, keepdims=True))
                rounded = probs.astype(jnp.bfloat16).astype(jnp.float32)
                delta = jnp.sum(rounded * dprobs[at], axis=-1, keepdims=True)
                dscores.append((probs * (dprobs[at] - delta) * SCALE).astype(jnp.bfloat16))
            if before is not None:
                pull_back(j, before)
        drot = dot(jnp.concatenate(dscores, axis=0), keys[:, head])
        for j in range(GROUP):
            part = drot[j * tokens : (j + 1) * tokens]
            turned = part * cosine[micro] - pltpu.roll(part, HEAD_DIM // 2, 1) * sine[micro]
            at = slice(j * HEAD_DIM, (j + 1) * HEAD_DIM)
            dq[:, at] = turned.astype(jnp.bfloat16)
        dquery[micro, :, columns(h)] = dq[...]
        middle_sum[...] += dot(dq[...], factor_bt[columns(h), :])

    @pl.when(h == 0)
    def _():
        if first:
            fetch(h).wait()
            project()
            for i in NEEDED_NEXT:
                stage(i).wait()
            upstream[...] = own[micro]
        attend()

    if first:

        @pl.when((h > 0) & (h + 1 < groups))
        def _():
            fetch(h + 1).start()

    @pl.when((h > 0) & (h < groups))
    def _():
        if first:
            fetch(h).wait()
            project()
        attend(dq[...])

    @pl.when(h == groups)
    def _():
        if first:
            for i in NEEDED_LAST:
                stage(i).wait()
        for piece in range(GROUP):
            pull_back(piece, dq[...])
        mid = middle_sum[...].astype(jnp.bfloat16)
        middle[micro] = mid
        dh = (total[...] + dot(mid, factor_a[...], NT)) * gain[...]
        scaled = rows_in[micro].astype(jnp.float32) * reciprocal[micro]
        mean = jnp.mean(dh * scaled, axis=1, keepdims=True)
        change = reciprocal[micro] * (dh - scaled * mean)
        share = change.shape[1] // len(order)
        for k, i in enumerate(order):
            here = slice(i * share, (i + 1) * share)
            result = upstream[:, here].astype(jnp.float32) + change[:, k * share : (k + 1) * share]
            input_gradient[:, here] = result.astype(jnp.bfloat16)
        grads[0] = input_gradient[...]


def backward(order, step, chosen, staged, weight, incoming, rotated, kept):
    first = step == 0
    own, keys, factor_a = staged[0], staged[3], staged[9]
    micros, tokens, features = own.shape
    width, rank = factor_a.shape
    ctx = keys.shape[0]
    rows = micros * tokens
    block = features // KV_HEADS
    untouched = pl.BlockSpec(memory_space=pl.ANY)
    in_vmem = pl.BlockSpec(memory_space=pltpu.VMEM)
    ins = [(in_hbm(a), untouched) if first else (a, in_vmem) for a in staged]
    ins.append((in_hbm(weight), untouched) if first else (weight, in_vmem))
    if incoming is not None:
        ins.append((incoming, in_vmem))
    if not first:
        ins.append((rotated, in_vmem))
    ins += [(a, in_vmem) for a in kept[:2]] + [(a, untouched) for a in kept[2:]]
    outs = [
        (
            pltpu.HBM((tokens, width), jnp.bfloat16),
            pl.BlockSpec((tokens, width), lambda h, m: (0, 0)),
        ),
        (pltpu.VMEM((micros, tokens, features), jnp.bfloat16), in_vmem),
        (pltpu.VMEM((micros, tokens, rank), jnp.bfloat16), in_vmem),
        (
            pltpu.HBM((micros, tokens, width), jnp.bfloat16),
            pl.BlockSpec((1, tokens, width), lambda h, m: (m[step], 0, 0)),
        ),
    ]
    scratch = [
        pltpu.VMEM((tokens, features), jnp.bfloat16),
        pltpu.VMEM((tokens, block), jnp.bfloat16),
        pltpu.VMEM((tokens, width), jnp.float32),
        pltpu.VMEM((tokens, rank), jnp.float32),
    ]
    if first:
        outs[:0] = [
            (pltpu.VMEM((KV_HEADS, width, block), jnp.bfloat16), in_vmem),
            (pltpu.VMEM((rows, features), jnp.bfloat16), in_vmem),
        ]
        outs += [(pltpu.VMEM(a.shape, a.dtype), in_vmem) for a in staged]
        scratch.append(pltpu.SemaphoreType.DMA((KV_HEADS,)))
        scratch.append(pltpu.SemaphoreType.DMA((len(staged),)))
        aliases = {}
    else:
        outs.append((pltpu.VMEM((KV_HEADS, width, block), jnp.bfloat16), in_vmem))
        at = len(staged)
        aliases = {1 + at: 4, len(ins) - 2: 1, len(ins) - 1: 2, len(ins): 3}
    return pl.pallas_call(
        functools.partial(step_kernel, order, step),
        grid_spec=pltpu.PrefetchScalarGridSpec(
            num_scalar_prefetch=1,
            grid=(KV_HEADS + 1,),
            in_specs=[spec for _, spec in ins],
            out_specs=[spec for _, spec in outs],
            scratch_shapes=scratch,
        ),
        out_shape=[shape for shape, _ in outs],
        input_output_aliases=aliases,
        compiler_params=pltpu.CompilerParams(vmem_limit_bytes=12 * 2**20),
        cost_estimate=pl.CostEstimate(
            flops=2 * tokens * features * (width + 3 * ctx),
            bytes_accessed=2 * width * features,
            transcendentals=tokens * HEADS * ctx,
        ),
        name="first_step" if first else "step",
    )(chosen, *(a for a, _ in ins))


def gradients_kernel(order, normed, middle, dquery, lowrank, out):
    flat = lambda ref: ref[...].reshape(normed.shape[0], ref.shape[-1])
    of_a = dot(flat(middle), normed[...], TN)
    of_bt = dot(lowrank[...], flat(dquery), TN)
    rank = of_a.shape[0]
    share = of_a.shape[1] // len(order)
    lanes = out.shape[2]
    for k, i in enumerate(order):
        for to, top, value in ((i, 0, of_a), (k, rank, of_bt)):
            mine = value[:, k * share : (k + 1) * share].astype(out.dtype)
            if share <= lanes:
                out[to, top : top + rank, :] = mine
                continue
            out[to, top : top + rank, :] = mine[:, :lanes]
            over = share - lanes
            side = lanes // over
            deep = rank // side
            folded = [mine[n * deep : (n + 1) * deep, lanes:] for n in range(side)]
            low = 2 * rank + top // side
            out[to, low : low + deep, :] = jnp.concatenate(folded, axis=1)


def gradients(order, normed, middle, dquery, lowrank):
    rows, width = normed.shape
    rank = middle.shape[-1]
    count = len(order)
    share = width // count
    lanes = min(share, HEAD_DIM)
    deep = 2 * rank * share // lanes
    return pl.pallas_call(
        functools.partial(gradients_kernel, order),
        in_specs=[pl.BlockSpec(memory_space=pltpu.VMEM)] * 4,
        out_shape=jax.ShapeDtypeStruct((count, deep, lanes), jnp.bfloat16),
        compiler_params=pltpu.CompilerParams(vmem_limit_bytes=12 * 2**20),
        name="gradients",
    )(normed, middle, dquery, lowrank)


def unfolded(total, rank, share):
    lanes = total.shape[1]
    if share == lanes:
        return total
    over = share - lanes
    side = lanes // over
    deep = rank // side
    parts = []
    for top in (0, rank):
        low = 2 * rank + top // side
        folded = total[low : low + deep]
        parts.append(
            jnp.concatenate([folded[:, n * over : (n + 1) * over] for n in range(side)], axis=0)
        )
    return jnp.concatenate([total[: 2 * rank], jnp.concatenate(parts, axis=0)], axis=1)


def gather_small(adapter_a, adapter_bt, norm_gain):
    count = lax.axis_size("dp")
    packed = jnp.concatenate([adapter_a, adapter_bt, norm_gain[:, None]], axis=1)
    sent = jnp.broadcast_to(packed[None], (count, *packed.shape))
    return lax.all_to_all(sent, "dp", split_axis=0, concat_axis=0, tiled=True)


def per_device(
    layer_inputs,
    top_grad,
    keys,
    values,
    query_weight,
    adapter_a,
    adapter_bt,
    norm_gain,
    offsets,
    segments,
):
    order = ring_order(lax.axis_size("dp"))
    _, _, micros, tokens, width = layer_inputs.shape
    rows = micros * tokens
    ctx = keys.shape[2]
    keys, values = keys[0, 0], values[0, 0]
    features = query_weight.shape[2]
    rank = adapter_a.shape[2]

    weight = lax.all_gather(
        query_weight[0], "dp", axis=0, tiled=True, axis_index_groups=[order]
    )
    small = gather_small(adapter_a[0], adapter_bt[0], norm_gain[0])
    factor_bt = small[:, :, rank : 2 * rank].reshape(features, rank)
    walked = jnp.concatenate([small[i : i + 1] for i in order], axis=0)
    factor_a = walked[:, :, :rank].reshape(width, rank)
    gain = walked[:, :, 2 * rank].reshape(1, width).astype(jnp.float32)

    rows_in = reordered(layer_inputs[0, 0], order)
    flat = rows_in.reshape(rows, width).astype(jnp.float32)
    reciprocal = lax.rsqrt(jnp.mean(flat * flat, axis=1, keepdims=True) + norm_eps)
    normed = (flat * reciprocal * gain).astype(jnp.bfloat16)
    lowrank = dot(normed, factor_a).astype(jnp.bfloat16)

    positions = (
        offsets[0][:, None] + jnp.arange(tokens, dtype=jnp.int32)[None, :]
    ).reshape(rows)
    seg_row = segments[0]
    place = jnp.arange(ctx, dtype=jnp.int32)
    query_seg = jnp.take(seg_row, positions)
    visible = (place[None, :] <= positions[:, None]) & (
        (seg_row[None, :] == 0) | (seg_row[None, :] == query_seg[:, None])
    )
    bias = jnp.where(visible, 0.0, -1e30).astype(jnp.float32)
    cosine, sine = rope_tables(positions)

    by_micro = lambda a: a.reshape(micros, tokens, a.shape[-1])
    section_count = lax.axis_size("pipe")
    section = lax.axis_index("pipe")
    last = section_count - 1
    steps = 2 * last + micros
    kept, arrived, rotated = (), [], None
    micro = jnp.clip(jnp.arange(steps) - 2 * (last - section), 0, micros - 1)
    chosen = jnp.append(micro, section == last).astype(jnp.int32)
    bias, cosine, sine, reciprocal = map(by_micro, (bias, cosine, sine, reciprocal))
    staged = [
        top_grad[0],
        normed,
        lowrank,
        keys,
        values,
        bias,
        cosine,
        sine,
        factor_bt,
        factor_a,
        rows_in,
        reciprocal,
        gain,
    ]
    for step in range(steps):
        incoming = arrived[step - 2] if step >= 2 else None
        made = list(backward(order, step, chosen, staged, weight, incoming, rotated, kept))
        if rotated is None:
            weight, rotated = made.pop(0), made.pop(0)
            made, staged = made[:4], made[4:]
        else:
            weight = made.pop()
        result, *kept = made
        if step < steps - 2:
            arrived.append(
                lax.ppermute(result, "pipe", [(s, s - 1) for s in range(1, section_count)])
            )

    grads = kept[2]
    partial = gradients(order, staged[1], kept[1], kept[0], staged[2])
    got = lax.all_to_all(partial, "dp", split_axis=0, concat_axis=0, tiled=True)
    total = unfolded(jnp.sum(got.astype(jnp.float32), axis=0), rank, width // len(order))
    return (grads[None, None], total[:rank].T[None], total[rank:].T[None])


def solution(mesh):
    placed = (
        P("pipe", "dp", None, None, None),
        P("dp", None, None, None),
        P("pipe", "dp", None, None),
        P("pipe", "dp", None, None),
        P("pipe", "dp", None),
        P("pipe", "dp", None),
        P("pipe", "dp", None),
        P("pipe", "dp"),
        P("dp", None),
        P("dp", None),
    )
    return jax.shard_map(
        per_device,
        mesh=mesh,
        in_specs=placed,
        out_specs=(
            P("pipe", "dp", None, None, None),
            P("pipe", "dp", None),
            P("pipe", "dp", None),
        ),
        check_vma=False,
    )
```

```python
import functools

import jax
import jax.numpy as jnp
from jax import lax
from jax.experimental import pallas as pl
from jax.experimental.pallas import tpu as pltpu
from jax.sharding import PartitionSpec as P

HEADS = 20
KV_HEADS = 4
HEAD_DIM = 128
GROUP = HEADS // KV_HEADS
CHUNK = 16

norm_eps = 1e-06
rope_base = 1000000.0
SCALE = 1.0 / HEAD_DIM**0.5

NT = (((1,), (1,)), ((), ()))
TN = (((0,), (0,)), ((), ()))


def dot(a, b, dims=(((1,), (0,)), ((), ()))):
    return lax.dot_general(a, b, dims, preferred_element_type=jnp.float32)


def rope_tables(positions):
    half = HEAD_DIM // 2
    expon = jnp.arange(half, dtype=jnp.float32) * (2.0 / HEAD_DIM)
    inverse = rope_base ** (-expon)
    angles = positions.astype(jnp.float32)[:, None] * inverse[None, :]
    cosine, sine = jnp.cos(angles), jnp.sin(angles)
    return (
        jnp.concatenate([cosine, cosine], axis=1),
        jnp.concatenate([-sine, sine], axis=1),
    )


def ring_order(count):
    if count % 4:
        return list(range(count))
    chips = count // 2
    columns = 2 ** ((chips.bit_length() - 1) // 2)
    lines = chips // columns
    walk = [(z, 0) for z in range(lines)]
    for step, z in enumerate(range(lines - 1, -1, -1)):
        side = range(1, columns) if step % 2 == 0 else range(columns - 1, 0, -1)
        walk += [(z, x) for x in side]
    return [(z * columns + x) * 2 + core for z, x in walk for core in range(2)]


def reordered(value, order):
    share = value.shape[-1] // len(order)
    return jnp.concatenate(
        [value[..., i * share : (i + 1) * share] for i in order], axis=-1
    )


def stacked(value):
    return jnp.concatenate(
        [value[:, j * HEAD_DIM : (j + 1) * HEAD_DIM] for j in range(GROUP)], axis=0
    )


NEEDED_FIRST = (1, 2, 8, 6, 7)
NEEDED_NEXT = (0, 3, 4, 5)
NEEDED_LAST = (9, 10, 11, 12)


def in_hbm(value):
    return pltpu.with_memory_space_constraint(value, pltpu.HBM)


def weight_pieces(shard, order):
    count = len(order)
    if count > 16 or count % 4:
        whole = lax.all_gather(shard, "dp", axis=0, tiled=True, axis_index_groups=[order])
        return [whole], jnp.zeros((1,), jnp.int32)
    chips = count // 2
    ahead = [
        (order[2 * k + core], order[2 * ((k + 1) % chips) + core])
        for k in range(chips)
        for core in range(2)
    ]
    behind = [(to, source) for source, to in ahead]
    pair = [(i, i ^ 1) for i in range(count)]
    table = jnp.array([order.index(i) for i in range(count)], jnp.int32)
    me = table[lax.axis_index("dp")]
    pieces, places = [shard], [me]
    forward = backward = shard
    for hop in range(1, chips // 2 + 1):
        forward = lax.ppermute(forward, "dp", ahead)
        pieces.append(forward)
        places.append((me - 2 * hop) % count)
        if hop <= (chips - 1) // 2:
            backward = lax.ppermute(backward, "dp", behind)
            pieces.append(backward)
            places.append((me + 2 * hop) % count)
    pieces += [lax.ppermute(piece, "dp", pair) for piece in pieces]
    places += [place ^ 1 for place in places]
    return pieces, jnp.stack(places)


def step_kernel(order, step, steps, chosen, *refs):
    first = step == 0
    refs = list(refs)
    given = arrays = refs[:13]
    incoming = refs[14] if step >= 2 else None
    if first:
        pieces = refs[13:-25]
        held, rotated, input_gradient, dquery, middle, grads = refs[-25:-19]
        staged = refs[-19:-6]
        sems, stage_sems = refs[-2:]
        upstream, dq, total, middle_sum = refs[-6:-2]
        stage = lambda i: pltpu.make_async_copy(given[i], staged[i], stage_sems.at[i])
        arrays = staged
    else:
        held = refs[13]
        rotated = refs[14 + (step >= 2)]
        input_gradient, dquery, middle, grads = refs[-9:-5]
        upstream, dq, total, middle_sum = refs[-4:]
    own, normed, lowrank, keys, values, bias, cosine, sine = arrays[:8]
    factor_bt, factor_a, rows_in, reciprocal, gain = arrays[8:]
    h = pl.program_id(0)
    groups = pl.num_programs(0) - 1
    micro = chosen[1 + step]
    tokens = bias.shape[1]
    width = gain.shape[1]
    block = GROUP * HEAD_DIM
    columns = lambda g: pl.ds(pl.multiple_of(g * block, HEAD_DIM), block)

    def fetch(g):
        copies = []
        for i, piece in enumerate(pieces):
            share = piece.shape[0]
            place = chosen[1 + steps + i] if len(pieces) > 1 else 0
            rows = pl.ds(pl.multiple_of(place * share, share), share)
            copies.append(
                pltpu.make_async_copy(
                    piece.at[:, columns(g)], held.at[g, rows, :], sems.at[g, i]
                )
            )
        return copies


    @pl.when(h == 0)
    def _():
        if first:
            for i in NEEDED_FIRST:
                stage(i).start()
            for copy in fetch(0):
                copy.start()
            for i in NEEDED_NEXT:
                stage(i).start()
            for copy in fetch(1):
                copy.start()
            for i in NEEDED_LAST:
                stage(i).start()
            for i in NEEDED_FIRST:
                stage(i).wait()
        total[...] = jnp.zeros_like(total)
        middle_sum[...] = jnp.zeros_like(middle_sum)
        if first:
            pass
        elif incoming is None:
            upstream[...] = own[micro]
        else:
            is_last = chosen[0] == 1
            upstream[...] = jnp.where(is_last, own[micro], incoming[...])

    def project():
        query = dot(normed[...], held[h]) + dot(lowrank[...], factor_bt[columns(h), :], NT)
        for m in range(rotated.shape[0] // tokens):
            rows = slice(m * tokens, (m + 1) * tokens)
            for j in range(GROUP):
                part = query[rows, j * HEAD_DIM : (j + 1) * HEAD_DIM]
                turned = part * cosine[m] + pltpu.roll(part, HEAD_DIM // 2, 1) * sine[m]
                at = pl.ds(pl.multiple_of(h * block + j * HEAD_DIM, HEAD_DIM), HEAD_DIM)
                rotated[rows, at] = turned.astype(jnp.bfloat16)

    def pull_back(piece, before):
        at = slice(piece * (width // GROUP), (piece + 1) * (width // GROUP))
        total[:, at] += dot(before, held[h - 1, at, :], NT)

    def attend(before=None):
        mine = rotated[pl.ds(pl.multiple_of(micro * tokens, tokens), tokens), columns(h)]
        head = pl.ds(pl.multiple_of(h * HEAD_DIM, HEAD_DIM), HEAD_DIM)
        scores = dot(stacked(mine), keys[:, head], NT)
        dprobs = dot(stacked(upstream[:, columns(h)]), values[:, head], NT)
        dscores = []
        for j in range(GROUP):
            for row in range(0, tokens, CHUNK):
                at = slice(j * tokens + row, j * tokens + row + CHUNK)
                masked = scores[at] * SCALE + bias[micro, row : row + CHUNK]
                expo = jnp.exp(masked - jnp.max(masked, axis=-1, keepdims=True))
                probs = expo * (1.0 / jnp.sum(expo, axis=-1, keepdims=True))
                rounded = probs.astype(jnp.bfloat16).astype(jnp.float32)
                delta = jnp.sum(rounded * dprobs[at], axis=-1, keepdims=True)
                dscores.append((probs * (dprobs[at] - delta) * SCALE).astype(jnp.bfloat16))
            if before is not None:
                pull_back(j, before)
        drot = dot(jnp.concatenate(dscores, axis=0), keys[:, head])
        for j in range(GROUP):
            part = drot[j * tokens : (j + 1) * tokens]
            turned = part * cosine[micro] - pltpu.roll(part, HEAD_DIM // 2, 1) * sine[micro]
            at = slice(j * HEAD_DIM, (j + 1) * HEAD_DIM)
            dq[:, at] = turned.astype(jnp.bfloat16)
        dquery[micro, :, columns(h)] = dq[...]
        middle_sum[...] += dot(dq[...], factor_bt[columns(h), :])

    @pl.when(h == 0)
    def _():
        if first:
            for copy in fetch(h):
                copy.wait()
            project()
            for i in NEEDED_NEXT:
                stage(i).wait()
            upstream[...] = own[micro]
        attend()

    if first:

        @pl.when((h > 0) & (h + 1 < groups))
        def _():
            for copy in fetch(h + 1):
                copy.start()

    @pl.when((h > 0) & (h < groups))
    def _():
        if first:
            for copy in fetch(h):
                copy.wait()
            project()
        attend(dq[...])

    @pl.when(h == groups)
    def _():
        if first:
            for i in NEEDED_LAST:
                stage(i).wait()
        for piece in range(GROUP):
            pull_back(piece, dq[...])
        mid = middle_sum[...].astype(jnp.bfloat16)
        middle[micro] = mid
        dh = (total[...] + dot(mid, factor_a[...], NT)) * gain[...]
        scaled = rows_in[micro].astype(jnp.float32) * reciprocal[micro]
        mean = jnp.mean(dh * scaled, axis=1, keepdims=True)
        change = reciprocal[micro] * (dh - scaled * mean)
        share = change.shape[1] // len(order)
        for k, i in enumerate(order):
            here = slice(i * share, (i + 1) * share)
            result = upstream[:, here].astype(jnp.float32) + change[:, k * share : (k + 1) * share]
            input_gradient[:, here] = result.astype(jnp.bfloat16)
        grads[0] = input_gradient[...]


def backward(order, step, steps, chosen, staged, weight, incoming, rotated, kept):
    first = step == 0
    own, keys, factor_a = staged[0], staged[3], staged[9]
    micros, tokens, features = own.shape
    width, rank = factor_a.shape
    ctx = keys.shape[0]
    rows = micros * tokens
    block = features // KV_HEADS
    untouched = pl.BlockSpec(memory_space=pl.ANY)
    in_vmem = pl.BlockSpec(memory_space=pltpu.VMEM)
    ins = [(in_hbm(a), untouched) if first else (a, in_vmem) for a in staged]
    ins += [(piece, untouched) for piece in weight] if first else [(weight, in_vmem)]
    if incoming is not None:
        ins.append((incoming, in_vmem))
    if not first:
        ins.append((rotated, in_vmem))
    ins += [(a, in_vmem) for a in kept[:2]] + [(a, untouched) for a in kept[2:]]
    outs = [
        (
            pltpu.HBM((tokens, width), jnp.bfloat16),
            pl.BlockSpec((tokens, width), lambda h, m: (0, 0)),
        ),
        (pltpu.VMEM((micros, tokens, features), jnp.bfloat16), in_vmem),
        (pltpu.VMEM((micros, tokens, rank), jnp.bfloat16), in_vmem),
        (
            pltpu.HBM((micros, tokens, width), jnp.bfloat16),
            pl.BlockSpec((1, tokens, width), lambda h, m: (m[1 + step], 0, 0)),
        ),
    ]
    scratch = [
        pltpu.VMEM((tokens, features), jnp.bfloat16),
        pltpu.VMEM((tokens, block), jnp.bfloat16),
        pltpu.VMEM((tokens, width), jnp.float32),
        pltpu.VMEM((tokens, rank), jnp.float32),
    ]
    if first:
        outs[:0] = [
            (pltpu.VMEM((KV_HEADS, width, block), jnp.bfloat16), in_vmem),
            (pltpu.VMEM((rows, features), jnp.bfloat16), in_vmem),
        ]
        outs += [(pltpu.VMEM(a.shape, a.dtype), in_vmem) for a in staged]
        scratch.append(pltpu.SemaphoreType.DMA((KV_HEADS, len(weight))))
        scratch.append(pltpu.SemaphoreType.DMA((len(staged),)))
        aliases = {}
    else:
        outs.append((pltpu.VMEM((KV_HEADS, width, block), jnp.bfloat16), in_vmem))
        at = len(staged)
        aliases = {1 + at: 4, len(ins) - 2: 1, len(ins) - 1: 2, len(ins): 3}
    return pl.pallas_call(
        functools.partial(step_kernel, order, step, steps),
        grid_spec=pltpu.PrefetchScalarGridSpec(
            num_scalar_prefetch=1,
            grid=(KV_HEADS + 1,),
            in_specs=[spec for _, spec in ins],
            out_specs=[spec for _, spec in outs],
            scratch_shapes=scratch,
        ),
        out_shape=[shape for shape, _ in outs],
        input_output_aliases=aliases,
        compiler_params=pltpu.CompilerParams(vmem_limit_bytes=12 * 2**20),
        cost_estimate=pl.CostEstimate(
            flops=2 * tokens * features * (width + 3 * ctx),
            bytes_accessed=2 * width * features,
            transcendentals=tokens * HEADS * ctx,
        ),
        name="first_step" if first else "step",
    )(chosen, *(a for a, _ in ins))


def gradients_kernel(order, normed, middle, dquery, lowrank, out):
    flat = lambda ref: ref[...].reshape(normed.shape[0], ref.shape[-1])
    of_a = dot(flat(middle), normed[...], TN)
    of_bt = dot(lowrank[...], flat(dquery), TN)
    rank = of_a.shape[0]
    share = of_a.shape[1] // len(order)
    lanes = out.shape[2]
    for k, i in enumerate(order):
        for to, top, value in ((i, 0, of_a), (k, rank, of_bt)):
            mine = value[:, k * share : (k + 1) * share].astype(out.dtype)
            if share <= lanes:
                out[to, top : top + rank, :] = mine
                continue
            out[to, top : top + rank, :] = mine[:, :lanes]
            over = share - lanes
            side = lanes // over
            deep = rank // side
            folded = [mine[n * deep : (n + 1) * deep, lanes:] for n in range(side)]
            low = 2 * rank + top // side
            out[to, low : low + deep, :] = jnp.concatenate(folded, axis=1)


def gradients(order, normed, middle, dquery, lowrank):
    rows, width = normed.shape
    rank = middle.shape[-1]
    count = len(order)
    share = width // count
    lanes = min(share, HEAD_DIM)
    deep = 2 * rank * share // lanes
    return pl.pallas_call(
        functools.partial(gradients_kernel, order),
        in_specs=[pl.BlockSpec(memory_space=pltpu.VMEM)] * 4,
        out_shape=jax.ShapeDtypeStruct((count, deep, lanes), jnp.bfloat16),
        compiler_params=pltpu.CompilerParams(vmem_limit_bytes=12 * 2**20),
        name="gradients",
    )(normed, middle, dquery, lowrank)


def unfolded(total, rank, share):
    lanes = total.shape[1]
    if share == lanes:
        return total
    over = share - lanes
    side = lanes // over
    deep = rank // side
    parts = []
    for top in (0, rank):
        low = 2 * rank + top // side
        folded = total[low : low + deep]
        parts.append(
            jnp.concatenate([folded[:, n * over : (n + 1) * over] for n in range(side)], axis=0)
        )
    return jnp.concatenate([total[: 2 * rank], jnp.concatenate(parts, axis=0)], axis=1)


def gather_small(adapter_a, adapter_bt, norm_gain):
    count = lax.axis_size("dp")
    packed = jnp.concatenate([adapter_a, adapter_bt, norm_gain[:, None]], axis=1)
    sent = jnp.broadcast_to(packed[None], (count, *packed.shape))
    return lax.all_to_all(sent, "dp", split_axis=0, concat_axis=0, tiled=True)


def per_device(
    layer_inputs,
    top_grad,
    keys,
    values,
    query_weight,
    adapter_a,
    adapter_bt,
    norm_gain,
    offsets,
    segments,
):
    order = ring_order(lax.axis_size("dp"))
    _, _, micros, tokens, width = layer_inputs.shape
    rows = micros * tokens
    ctx = keys.shape[2]
    keys, values = keys[0, 0], values[0, 0]
    features = query_weight.shape[2]
    rank = adapter_a.shape[2]

    weight, places = weight_pieces(query_weight[0], order)
    small = gather_small(adapter_a[0], adapter_bt[0], norm_gain[0])
    factor_bt = small[:, :, rank : 2 * rank].reshape(features, rank)
    walked = jnp.concatenate([small[i : i + 1] for i in order], axis=0)
    factor_a = walked[:, :, :rank].reshape(width, rank)
    gain = walked[:, :, 2 * rank].reshape(1, width).astype(jnp.float32)

    rows_in = reordered(layer_inputs[0, 0], order)
    flat = rows_in.reshape(rows, width).astype(jnp.float32)
    reciprocal = lax.rsqrt(jnp.mean(flat * flat, axis=1, keepdims=True) + norm_eps)
    normed = (flat * reciprocal * gain).astype(jnp.bfloat16)
    lowrank = dot(normed, factor_a).astype(jnp.bfloat16)

    positions = (
        offsets[0][:, None] + jnp.arange(tokens, dtype=jnp.int32)[None, :]
    ).reshape(rows)
    seg_row = segments[0]
    place = jnp.arange(ctx, dtype=jnp.int32)
    query_seg = jnp.take(seg_row, positions)
    visible = (place[None, :] <= positions[:, None]) & (
        (seg_row[None, :] == 0) | (seg_row[None, :] == query_seg[:, None])
    )
    bias = jnp.where(visible, 0.0, -1e30).astype(jnp.float32)
    cosine, sine = rope_tables(positions)

    by_micro = lambda a: a.reshape(micros, tokens, a.shape[-1])
    section_count = lax.axis_size("pipe")
    section = lax.axis_index("pipe")
    last = section_count - 1
    steps = 2 * last + micros
    kept, arrived, rotated = (), [], None
    micro = jnp.clip(jnp.arange(steps) - 2 * (last - section), 0, micros - 1)
    is_last = jnp.reshape(section == last, 1).astype(jnp.int32)
    chosen = jnp.concatenate([is_last, micro.astype(jnp.int32), places])
    bias, cosine, sine, reciprocal = map(by_micro, (bias, cosine, sine, reciprocal))
    staged = [
        top_grad[0],
        normed,
        lowrank,
        keys,
        values,
        bias,
        cosine,
        sine,
        factor_bt,
        factor_a,
        rows_in,
        reciprocal,
        gain,
    ]
    for step in range(steps):
        incoming = arrived[step - 2] if step >= 2 else None
        made = list(backward(order, step, steps, chosen, staged, weight, incoming, rotated, kept))
        if rotated is None:
            weight, rotated = made.pop(0), made.pop(0)
            made, staged = made[:4], made[4:]
        else:
            weight = made.pop()
        result, *kept = made
        if step < steps - 2:
            arrived.append(
                lax.ppermute(result, "pipe", [(s, s - 1) for s in range(1, section_count)])
            )

    grads = kept[2]
    partial = gradients(order, staged[1], kept[1], kept[0], staged[2])
    got = lax.all_to_all(partial, "dp", split_axis=0, concat_axis=0, tiled=True)
    total = unfolded(jnp.sum(got.astype(jnp.float32), axis=0), rank, width // len(order))
    return (grads[None, None], total[:rank].T[None], total[rank:].T[None])


def solution(mesh):
    placed = (
        P("pipe", "dp", None, None, None),
        P("dp", None, None, None),
        P("pipe", "dp", None, None),
        P("pipe", "dp", None, None),
        P("pipe", "dp", None),
        P("pipe", "dp", None),
        P("pipe", "dp", None),
        P("pipe", "dp"),
        P("dp", None),
        P("dp", None),
    )
    return jax.shard_map(
        per_device,
        mesh=mesh,
        in_specs=placed,
        out_specs=(
            P("pipe", "dp", None, None, None),
            P("pipe", "dp", None),
            P("pipe", "dp", None),
        ),
        check_vma=False,
    )
```

```python
import functools

import jax
import jax.numpy as jnp
from jax import lax
from jax.experimental import pallas as pl
from jax.experimental.pallas import tpu as pltpu
from jax.sharding import PartitionSpec as P

HEADS = 20
KV_HEADS = 4
HEAD_DIM = 128
GROUP = HEADS // KV_HEADS
CHUNK = 16

norm_eps = 1e-06
rope_base = 1000000.0
SCALE = 1.0 / HEAD_DIM**0.5

NT = (((1,), (1,)), ((), ()))
TN = (((0,), (0,)), ((), ()))


def dot(a, b, dims=(((1,), (0,)), ((), ()))):
    return lax.dot_general(a, b, dims, preferred_element_type=jnp.float32)


def rope_tables(positions):
    half = HEAD_DIM // 2
    expon = jnp.arange(half, dtype=jnp.float32) * (2.0 / HEAD_DIM)
    inverse = rope_base ** (-expon)
    angles = positions.astype(jnp.float32)[:, None] * inverse[None, :]
    cosine, sine = jnp.cos(angles), jnp.sin(angles)
    return (
        jnp.concatenate([cosine, cosine], axis=1),
        jnp.concatenate([-sine, sine], axis=1),
    )


def ring_order(count):
    if count % 4:
        return list(range(count))
    chips = count // 2
    columns = 2 ** ((chips.bit_length() - 1) // 2)
    lines = chips // columns
    walk = [(z, 0) for z in range(lines)]
    for step, z in enumerate(range(lines - 1, -1, -1)):
        side = range(1, columns) if step % 2 == 0 else range(columns - 1, 0, -1)
        walk += [(z, x) for x in side]
    return [(z * columns + x) * 2 + core for z, x in walk for core in range(2)]


def reordered(value, order):
    share = value.shape[-1] // len(order)
    return jnp.concatenate(
        [value[..., i * share : (i + 1) * share] for i in order], axis=-1
    )


def stacked(value):
    return jnp.concatenate(
        [value[:, j * HEAD_DIM : (j + 1) * HEAD_DIM] for j in range(GROUP)], axis=0
    )


NEEDED_FIRST = (1, 2, 8, 6, 7)
NEEDED_NEXT = (0, 3, 4, 5)
NEEDED_LAST = (9, 10, 11, 12)


def in_hbm(value):
    return pltpu.with_memory_space_constraint(value, pltpu.HBM)


def places_of(order):
    count = len(order)
    if count > 16 or count % 4:
        return jnp.zeros((1,), jnp.int32)
    chips = count // 2
    table = jnp.array([order.index(i) for i in range(count)], jnp.int32)
    hops = [0]
    for hop in range(1, chips // 2 + 1):
        hops += [-hop, hop] if hop <= (chips - 1) // 2 else [-hop]
    own = (table[lax.axis_index("dp")] + 2 * jnp.array(hops, jnp.int32)) % count
    return jnp.concatenate([own, own ^ 1])


def weight_pieces(shard, order, early, small, make_late):
    count = len(order)
    if count > 16 or count % 4:
        whole = lax.all_gather(shard, "dp", axis=0, tiled=True, axis_index_groups=[order])
        return [whole], early, make_late(small)
    chips = count // 2
    ahead = [
        (order[2 * k + core], order[2 * ((k + 1) % chips) + core])
        for k in range(chips)
        for core in range(2)
    ]
    behind = [(to, source) for source, to in ahead]
    pair = [(i, i ^ 1) for i in range(count)]
    pieces = [shard]
    forward = backward = shard
    for hop in range(1, chips // 2 + 1):
        if hop == 2:
            forward, backward, early = lax.optimization_barrier((forward, backward, early))
        if hop == chips // 2 - 1:
            forward, backward, small = lax.optimization_barrier((forward, backward, small))
            late = make_late(small)
        if hop == chips // 2:
            forward, late = lax.optimization_barrier((forward, late))
        forward = lax.ppermute(forward, "dp", ahead)
        pieces.append(forward)
        if hop <= (chips - 1) // 2:
            backward = lax.ppermute(backward, "dp", behind)
            pieces.append(backward)
    pieces += [lax.ppermute(piece, "dp", pair) for piece in pieces]
    return pieces, early, late


def step_kernel(order, step, steps, chosen, *refs):
    first = step == 0
    refs = list(refs)
    given = arrays = refs[:13]
    incoming = refs[14] if step >= 2 else None
    if first:
        pieces = refs[13:-25]
        held, rotated, input_gradient, dquery, middle, grads = refs[-25:-19]
        staged = refs[-19:-6]
        sems, stage_sems = refs[-2:]
        upstream, dq, total, middle_sum = refs[-6:-2]
        stage = lambda i: pltpu.make_async_copy(given[i], staged[i], stage_sems.at[i])
        arrays = staged
    else:
        held = refs[13]
        rotated = refs[14 + (step >= 2)]
        input_gradient, dquery, middle, grads = refs[-9:-5]
        upstream, dq, total, middle_sum = refs[-4:]
    own, normed, lowrank, keys, values, bias, cosine, sine = arrays[:8]
    factor_bt, factor_a, rows_in, reciprocal, gain = arrays[8:]
    h = pl.program_id(0)
    groups = pl.num_programs(0) - 1
    micro = chosen[1 + step]
    tokens = bias.shape[1]
    width = gain.shape[1]
    block = GROUP * HEAD_DIM
    columns = lambda g: pl.ds(pl.multiple_of(g * block, HEAD_DIM), block)

    def fetch(g):
        copies = []
        for i, piece in enumerate(pieces):
            share = piece.shape[0]
            place = chosen[1 + steps + i] if len(pieces) > 1 else 0
            rows = pl.ds(pl.multiple_of(place * share, share), share)
            copies.append(
                pltpu.make_async_copy(
                    piece.at[:, columns(g)], held.at[g, rows, :], sems.at[g, i]
                )
            )
        return copies


    @pl.when(h == 0)
    def _():
        if first:
            for i in NEEDED_FIRST:
                stage(i).start()
            for copy in fetch(0):
                copy.start()
            for i in NEEDED_NEXT:
                stage(i).start()
            for copy in fetch(1):
                copy.start()
            for i in NEEDED_LAST:
                stage(i).start()
            for i in NEEDED_FIRST:
                stage(i).wait()
        total[...] = jnp.zeros_like(total)
        middle_sum[...] = jnp.zeros_like(middle_sum)
        if first:
            pass
        elif incoming is None:
            upstream[...] = own[micro]
        else:
            is_last = chosen[0] == 1
            upstream[...] = jnp.where(is_last, own[micro], incoming[...])

    def project():
        query = dot(normed[...], held[h]) + dot(lowrank[...], factor_bt[columns(h), :], NT)
        for m in range(rotated.shape[0] // tokens):
            rows = slice(m * tokens, (m + 1) * tokens)
            for j in range(GROUP):
                part = query[rows, j * HEAD_DIM : (j + 1) * HEAD_DIM]
                turned = part * cosine[m] + pltpu.roll(part, HEAD_DIM // 2, 1) * sine[m]
                at = pl.ds(pl.multiple_of(h * block + j * HEAD_DIM, HEAD_DIM), HEAD_DIM)
                rotated[rows, at] = turned.astype(jnp.bfloat16)

    def pull_back(piece, before):
        at = slice(piece * (width // GROUP), (piece + 1) * (width // GROUP))
        total[:, at] += dot(before, held[h - 1, at, :], NT)

    def attend(before=None):
        mine = rotated[pl.ds(pl.multiple_of(micro * tokens, tokens), tokens), columns(h)]
        head = pl.ds(pl.multiple_of(h * HEAD_DIM, HEAD_DIM), HEAD_DIM)
        scores = dot(stacked(mine), keys[:, head], NT)
        dprobs = dot(stacked(upstream[:, columns(h)]), values[:, head], NT)
        dscores = []
        for j in range(GROUP):
            for row in range(0, tokens, CHUNK):
                at = slice(j * tokens + row, j * tokens + row + CHUNK)
                masked = scores[at] * SCALE + bias[micro, row : row + CHUNK]
                expo = jnp.exp(masked - jnp.max(masked, axis=-1, keepdims=True))
                probs = expo * (1.0 / jnp.sum(expo, axis=-1, keepdims=True))
                rounded = probs.astype(jnp.bfloat16).astype(jnp.float32)
                delta = jnp.sum(rounded * dprobs[at], axis=-1, keepdims=True)
                dscores.append((probs * (dprobs[at] - delta) * SCALE).astype(jnp.bfloat16))
            if before is not None:
                pull_back(j, before)
        drot = dot(jnp.concatenate(dscores, axis=0), keys[:, head])
        for j in range(GROUP):
            part = drot[j * tokens : (j + 1) * tokens]
            turned = part * cosine[micro] - pltpu.roll(part, HEAD_DIM // 2, 1) * sine[micro]
            at = slice(j * HEAD_DIM, (j + 1) * HEAD_DIM)
            dq[:, at] = turned.astype(jnp.bfloat16)
        dquery[micro, :, columns(h)] = dq[...]
        middle_sum[...] += dot(dq[...], factor_bt[columns(h), :])

    @pl.when(h == 0)
    def _():
        if first:
            for copy in fetch(h):
                copy.wait()
            project()
            for i in NEEDED_NEXT:
                stage(i).wait()
            upstream[...] = own[micro]
        attend()

    if first:

        @pl.when((h > 0) & (h + 1 < groups))
        def _():
            for copy in fetch(h + 1):
                copy.start()

    @pl.when((h > 0) & (h < groups))
    def _():
        if first:
            for copy in fetch(h):
                copy.wait()
            project()
        attend(dq[...])

    @pl.when(h == groups)
    def _():
        if first:
            for i in NEEDED_LAST:
                stage(i).wait()
        for piece in range(GROUP):
            pull_back(piece, dq[...])
        mid = middle_sum[...].astype(jnp.bfloat16)
        middle[micro] = mid
        dh = (total[...] + dot(mid, factor_a[...], NT)) * gain[...]
        scaled = rows_in[micro].astype(jnp.float32) * reciprocal[micro]
        mean = jnp.mean(dh * scaled, axis=1, keepdims=True)
        change = reciprocal[micro] * (dh - scaled * mean)
        share = change.shape[1] // len(order)
        for k, i in enumerate(order):
            here = slice(i * share, (i + 1) * share)
            result = upstream[:, here].astype(jnp.float32) + change[:, k * share : (k + 1) * share]
            input_gradient[:, here] = result.astype(jnp.bfloat16)
        grads[0] = input_gradient[...]


def backward(order, step, steps, chosen, staged, weight, incoming, rotated, kept):
    first = step == 0
    own, keys, factor_a = staged[0], staged[3], staged[9]
    micros, tokens, features = own.shape
    width, rank = factor_a.shape
    ctx = keys.shape[0]
    rows = micros * tokens
    block = features // KV_HEADS
    untouched = pl.BlockSpec(memory_space=pl.ANY)
    in_vmem = pl.BlockSpec(memory_space=pltpu.VMEM)
    ins = [(in_hbm(a), untouched) if first else (a, in_vmem) for a in staged]
    ins += [(piece, untouched) for piece in weight] if first else [(weight, in_vmem)]
    if incoming is not None:
        ins.append((incoming, in_vmem))
    if not first:
        ins.append((rotated, in_vmem))
    ins += [(a, in_vmem) for a in kept[:2]] + [(a, untouched) for a in kept[2:]]
    outs = [
        (
            pltpu.HBM((tokens, width), jnp.bfloat16),
            pl.BlockSpec((tokens, width), lambda h, m: (0, 0)),
        ),
        (pltpu.VMEM((micros, tokens, features), jnp.bfloat16), in_vmem),
        (pltpu.VMEM((micros, tokens, rank), jnp.bfloat16), in_vmem),
        (
            pltpu.HBM((micros, tokens, width), jnp.bfloat16),
            pl.BlockSpec((1, tokens, width), lambda h, m: (m[1 + step], 0, 0)),
        ),
    ]
    scratch = [
        pltpu.VMEM((tokens, features), jnp.bfloat16),
        pltpu.VMEM((tokens, block), jnp.bfloat16),
        pltpu.VMEM((tokens, width), jnp.float32),
        pltpu.VMEM((tokens, rank), jnp.float32),
    ]
    if first:
        outs[:0] = [
            (pltpu.VMEM((KV_HEADS, width, block), jnp.bfloat16), in_vmem),
            (pltpu.VMEM((rows, features), jnp.bfloat16), in_vmem),
        ]
        outs += [(pltpu.VMEM(a.shape, a.dtype), in_vmem) for a in staged]
        scratch.append(pltpu.SemaphoreType.DMA((KV_HEADS, len(weight))))
        scratch.append(pltpu.SemaphoreType.DMA((len(staged),)))
        aliases = {}
    else:
        outs.append((pltpu.VMEM((KV_HEADS, width, block), jnp.bfloat16), in_vmem))
        at = len(staged)
        aliases = {1 + at: 4, len(ins) - 2: 1, len(ins) - 1: 2, len(ins): 3}
    return pl.pallas_call(
        functools.partial(step_kernel, order, step, steps),
        grid_spec=pltpu.PrefetchScalarGridSpec(
            num_scalar_prefetch=1,
            grid=(KV_HEADS + 1,),
            in_specs=[spec for _, spec in ins],
            out_specs=[spec for _, spec in outs],
            scratch_shapes=scratch,
        ),
        out_shape=[shape for shape, _ in outs],
        input_output_aliases=aliases,
        compiler_params=pltpu.CompilerParams(vmem_limit_bytes=12 * 2**20),
        cost_estimate=pl.CostEstimate(
            flops=2 * tokens * features * (width + 3 * ctx),
            bytes_accessed=2 * width * features,
            transcendentals=tokens * HEADS * ctx,
        ),
        name="first_step" if first else "step",
    )(chosen, *(a for a, _ in ins))


def gradients_kernel(order, normed, middle, dquery, lowrank, out):
    flat = lambda ref: ref[...].reshape(normed.shape[0], ref.shape[-1])
    of_a = dot(flat(middle), normed[...], TN)
    of_bt = dot(lowrank[...], flat(dquery), TN)
    rank = of_a.shape[0]
    share = of_a.shape[1] // len(order)
    lanes = out.shape[2]
    for k, i in enumerate(order):
        for to, top, value in ((i, 0, of_a), (k, rank, of_bt)):
            mine = value[:, k * share : (k + 1) * share].astype(out.dtype)
            if share <= lanes:
                out[to, top : top + rank, :] = mine
                continue
            out[to, top : top + rank, :] = mine[:, :lanes]
            over = share - lanes
            side = lanes // over
            deep = rank // side
            folded = [mine[n * deep : (n + 1) * deep, lanes:] for n in range(side)]
            low = 2 * rank + top // side
            out[to, low : low + deep, :] = jnp.concatenate(folded, axis=1)


def gradients(order, normed, middle, dquery, lowrank):
    rows, width = normed.shape
    rank = middle.shape[-1]
    count = len(order)
    share = width // count
    lanes = min(share, HEAD_DIM)
    deep = 2 * rank * share // lanes
    return pl.pallas_call(
        functools.partial(gradients_kernel, order),
        in_specs=[pl.BlockSpec(memory_space=pltpu.VMEM)] * 4,
        out_shape=jax.ShapeDtypeStruct((count, deep, lanes), jnp.bfloat16),
        compiler_params=pltpu.CompilerParams(vmem_limit_bytes=12 * 2**20),
        name="gradients",
    )(normed, middle, dquery, lowrank)


def unfolded(total, rank, share):
    lanes = total.shape[1]
    if share == lanes:
        return total
    over = share - lanes
    side = lanes // over
    deep = rank // side
    parts = []
    for top in (0, rank):
        low = 2 * rank + top // side
        folded = total[low : low + deep]
        parts.append(
            jnp.concatenate([folded[:, n * over : (n + 1) * over] for n in range(side)], axis=0)
        )
    return jnp.concatenate([total[: 2 * rank], jnp.concatenate(parts, axis=0)], axis=1)


def gather_small(adapter_a, adapter_bt, norm_gain):
    count = lax.axis_size("dp")
    packed = jnp.concatenate([adapter_a, adapter_bt, norm_gain[:, None]], axis=1)
    sent = jnp.broadcast_to(packed[None], (count, *packed.shape))
    return lax.all_to_all(sent, "dp", split_axis=0, concat_axis=0, tiled=True)


def per_device(
    layer_inputs,
    top_grad,
    keys,
    values,
    query_weight,
    adapter_a,
    adapter_bt,
    norm_gain,
    offsets,
    segments,
):
    order = ring_order(lax.axis_size("dp"))
    _, _, micros, tokens, width = layer_inputs.shape
    rows = micros * tokens
    ctx = keys.shape[2]
    keys, values = keys[0, 0], values[0, 0]
    features = query_weight.shape[2]
    rank = adapter_a.shape[2]

    small = gather_small(adapter_a[0], adapter_bt[0], norm_gain[0])
    rows_in = reordered(layer_inputs[0, 0], order)
    flat = rows_in.reshape(rows, width).astype(jnp.float32)
    reciprocal = lax.rsqrt(jnp.mean(flat * flat, axis=1, keepdims=True) + norm_eps)

    def make_late(given):
        small, rows_in, reciprocal = given
        factor_bt = small[:, :, rank : 2 * rank].reshape(features, rank)
        walked = jnp.concatenate([small[i : i + 1] for i in order], axis=0)
        factor_a = walked[:, :, :rank].reshape(width, rank)
        gain = walked[:, :, 2 * rank].reshape(1, width).astype(jnp.float32)
        flat = rows_in.reshape(rows, width).astype(jnp.float32)
        normed = (flat * reciprocal * gain).astype(jnp.bfloat16)
        lowrank = dot(normed, factor_a).astype(jnp.bfloat16)
        return normed, lowrank, factor_bt, factor_a, gain

    positions = (
        offsets[0][:, None] + jnp.arange(tokens, dtype=jnp.int32)[None, :]
    ).reshape(rows)
    seg_row = segments[0]
    place = jnp.arange(ctx, dtype=jnp.int32)
    query_seg = jnp.take(seg_row, positions)
    visible = (place[None, :] <= positions[:, None]) & (
        (seg_row[None, :] == 0) | (seg_row[None, :] == query_seg[:, None])
    )
    bias = jnp.where(visible, 0.0, -1e30).astype(jnp.float32)
    cosine, sine = rope_tables(positions)

    by_micro = lambda a: a.reshape(micros, tokens, a.shape[-1])
    section_count = lax.axis_size("pipe")
    section = lax.axis_index("pipe")
    last = section_count - 1
    steps = 2 * last + micros
    kept, arrived, rotated = (), [], None
    micro = jnp.clip(jnp.arange(steps) - 2 * (last - section), 0, micros - 1)
    is_last = jnp.reshape(section == last, 1).astype(jnp.int32)
    chosen = jnp.concatenate([is_last, micro.astype(jnp.int32), places_of(order)])
    given = small, rows_in, reciprocal
    early = (chosen, *map(by_micro, (bias, cosine, sine, reciprocal)))
    weight, early, late = weight_pieces(query_weight[0], order, early, given, make_late)
    chosen, bias, cosine, sine, reciprocal = early
    normed, lowrank, factor_bt, factor_a, gain = late
    staged = [
        top_grad[0],
        normed,
        lowrank,
        keys,
        values,
        bias,
        cosine,
        sine,
        factor_bt,
        factor_a,
        rows_in,
        reciprocal,
        gain,
    ]
    for step in range(steps):
        incoming = arrived[step - 2] if step >= 2 else None
        made = list(backward(order, step, steps, chosen, staged, weight, incoming, rotated, kept))
        if rotated is None:
            weight, rotated = made.pop(0), made.pop(0)
            made, staged = made[:4], made[4:]
        else:
            weight = made.pop()
        result, *kept = made
        if step < steps - 2:
            arrived.append(
                lax.ppermute(result, "pipe", [(s, s - 1) for s in range(1, section_count)])
            )

    grads = kept[2]
    partial = gradients(order, staged[1], kept[1], kept[0], staged[2])
    got = lax.all_to_all(partial, "dp", split_axis=0, concat_axis=0, tiled=True)
    total = unfolded(jnp.sum(got.astype(jnp.float32), axis=0), rank, width // len(order))
    return (grads[None, None], total[:rank].T[None], total[rank:].T[None])


def solution(mesh):
    placed = (
        P("pipe", "dp", None, None, None),
        P("dp", None, None, None),
        P("pipe", "dp", None, None),
        P("pipe", "dp", None, None),
        P("pipe", "dp", None),
        P("pipe", "dp", None),
        P("pipe", "dp", None),
        P("pipe", "dp"),
        P("dp", None),
        P("dp", None),
    )
    return jax.shard_map(
        per_device,
        mesh=mesh,
        in_specs=placed,
        out_specs=(
            P("pipe", "dp", None, None, None),
            P("pipe", "dp", None),
            P("pipe", "dp", None),
        ),
        check_vma=False,
    )
```

```python
import functools

import jax
import jax.numpy as jnp
from jax import lax
from jax.experimental import pallas as pl
from jax.experimental.pallas import tpu as pltpu
from jax.sharding import PartitionSpec as P

HEADS = 20
KV_HEADS = 4
HEAD_DIM = 128
GROUP = HEADS // KV_HEADS
CHUNK = 16

norm_eps = 1e-06
rope_base = 1000000.0
SCALE = 1.0 / HEAD_DIM**0.5

NT = (((1,), (1,)), ((), ()))
TN = (((0,), (0,)), ((), ()))


def dot(a, b, dims=(((1,), (0,)), ((), ()))):
    return lax.dot_general(a, b, dims, preferred_element_type=jnp.float32)


def rope_tables(positions):
    half = HEAD_DIM // 2
    expon = jnp.arange(half, dtype=jnp.float32) * (2.0 / HEAD_DIM)
    inverse = rope_base ** (-expon)
    angles = positions.astype(jnp.float32)[:, None] * inverse[None, :]
    cosine, sine = jnp.cos(angles), jnp.sin(angles)
    return (
        jnp.concatenate([cosine, cosine], axis=1),
        jnp.concatenate([-sine, sine], axis=1),
    )


def ring_order(count):
    if count % 4:
        return list(range(count))
    chips = count // 2
    columns = 2 ** ((chips.bit_length() - 1) // 2)
    lines = chips // columns
    walk = [(z, 0) for z in range(lines)]
    for step, z in enumerate(range(lines - 1, -1, -1)):
        side = range(1, columns) if step % 2 == 0 else range(columns - 1, 0, -1)
        walk += [(z, x) for x in side]
    return [(z * columns + x) * 2 + core for z, x in walk for core in range(2)]


def reordered(value, order):
    share = value.shape[-1] // len(order)
    return jnp.concatenate(
        [value[..., i * share : (i + 1) * share] for i in order], axis=-1
    )


def stacked(value):
    return jnp.concatenate(
        [value[:, j * HEAD_DIM : (j + 1) * HEAD_DIM] for j in range(GROUP)], axis=0
    )


NEEDED_FIRST = (1, 2, 8, 6, 7)
NEEDED_NEXT = (0, 3, 4, 5)
NEEDED_LAST = (9, 10, 11, 12)
OF_FEATURES = 8


def in_hbm(value):
    return pltpu.with_memory_space_constraint(value, pltpu.HBM)


def places_of(order):
    count = len(order)
    if count != 16:
        return jnp.zeros((1,), jnp.int32)
    chips = count // 2
    table = jnp.array([order.index(i) for i in range(count)], jnp.int32)
    hops = [0]
    for hop in range(1, chips // 2 + 1):
        hops += [-hop, hop] if hop <= (chips - 1) // 2 else [-hop]
    own = (table[lax.axis_index("dp")] + 2 * jnp.array(hops, jnp.int32)) % count
    return jnp.concatenate([own, own ^ 1])


def weight_pieces(shard, order, early, small, make_late):
    count = len(order)
    if count != 16:
        whole = lax.all_gather(shard, "dp", axis=0, tiled=True, axis_index_groups=[order])
        return [whole], early, make_late(small)
    chips = count // 2
    ahead = [
        (order[2 * k + core], order[2 * ((k + 1) % chips) + core])
        for k in range(chips)
        for core in range(2)
    ]
    behind = [(to, source) for source, to in ahead]
    pair = [(i, i ^ 1) for i in range(count)]
    pieces = [shard]
    forward = backward = shard
    for hop in range(1, chips // 2 + 1):
        if hop == 2:
            tied = (forward, backward, early, small)
            forward, backward, early, small = lax.optimization_barrier(tied)
            late = make_late(small)
        if hop == 3:
            forward, backward, late = lax.optimization_barrier((forward, backward, late))
        forward = lax.ppermute(forward, "dp", ahead)
        pieces.append(forward)
        if hop <= (chips - 1) // 2:
            backward = lax.ppermute(backward, "dp", behind)
            pieces.append(backward)
    pieces += [lax.ppermute(piece, "dp", pair) for piece in pieces]
    return pieces, early, late


def step_kernel(order, step, steps, chosen, *refs):
    first = step == 0
    refs = list(refs)
    given = arrays = refs[:13]
    incoming = refs[14] if step >= 2 else None
    if first:
        pieces = refs[13:-25]
        held, rotated, input_gradient, dquery, middle, grads = refs[-25:-19]
        staged = refs[-19:-6]
        sems, stage_sems = refs[-2:]
        upstream, dq, total, middle_sum = refs[-6:-2]
        arrays = staged

        def stage(i):
            if i != OF_FEATURES:
                return [pltpu.make_async_copy(given[i], staged[i], stage_sems.at[i])]
            share = given[i].shape[0] // len(order)
            return [
                pltpu.make_async_copy(
                    given[i].at[k * share : (k + 1) * share],
                    staged[i].at[to * share : (to + 1) * share],
                    stage_sems.at[len(given) + k],
                )
                for k, to in enumerate(order)
            ]

    else:
        held = refs[13]
        rotated = refs[14 + (step >= 2)]
        input_gradient, dquery, middle, grads = refs[-9:-5]
        upstream, dq, total, middle_sum = refs[-4:]
    own, normed, lowrank, keys, values, bias, cosine, sine = arrays[:8]
    factor_bt, factor_a, rows_in, reciprocal, gain = arrays[8:]
    h = pl.program_id(0)
    groups = pl.num_programs(0) - 1
    micro = chosen[1 + step]
    tokens = bias.shape[1]
    width = gain.shape[1]
    block = GROUP * HEAD_DIM
    columns = lambda g: pl.ds(pl.multiple_of(g * block, HEAD_DIM), block)

    def fetch(g):
        copies = []
        for i, piece in enumerate(pieces):
            share = piece.shape[0]
            place = chosen[1 + steps + i] if len(pieces) > 1 else 0
            rows = pl.ds(pl.multiple_of(place * share, share), share)
            copies.append(
                pltpu.make_async_copy(
                    piece.at[:, columns(g)], held.at[g, rows, :], sems.at[g, i]
                )
            )
        return copies


    @pl.when(h == 0)
    def _():
        if first:
            for i in NEEDED_FIRST:
                for copy in stage(i):
                    copy.start()
            for copy in fetch(0):
                copy.start()
            for i in NEEDED_NEXT:
                for copy in stage(i):
                    copy.start()
            for copy in fetch(1):
                copy.start()
            for i in NEEDED_LAST:
                for copy in stage(i):
                    copy.start()
            for i in NEEDED_FIRST:
                for copy in stage(i):
                    copy.wait()
        total[...] = jnp.zeros_like(total)
        middle_sum[...] = jnp.zeros_like(middle_sum)
        if first:
            pass
        elif incoming is None:
            upstream[...] = own[micro]
        else:
            is_last = chosen[0] == 1
            upstream[...] = jnp.where(is_last, own[micro], incoming[...])

    def project():
        query = dot(normed[...], held[h]) + dot(lowrank[...], factor_bt[columns(h), :], NT)
        for m in range(rotated.shape[0] // tokens):
            rows = slice(m * tokens, (m + 1) * tokens)
            for j in range(GROUP):
                part = query[rows, j * HEAD_DIM : (j + 1) * HEAD_DIM]
                turned = part * cosine[m] + pltpu.roll(part, HEAD_DIM // 2, 1) * sine[m]
                at = pl.ds(pl.multiple_of(h * block + j * HEAD_DIM, HEAD_DIM), HEAD_DIM)
                rotated[rows, at] = turned.astype(jnp.bfloat16)

    def pull_back(piece, before):
        at = slice(piece * (width // GROUP), (piece + 1) * (width // GROUP))
        total[:, at] += dot(before, held[h - 1, at, :], NT)

    def attend(before=None):
        mine = rotated[pl.ds(pl.multiple_of(micro * tokens, tokens), tokens), columns(h)]
        head = pl.ds(pl.multiple_of(h * HEAD_DIM, HEAD_DIM), HEAD_DIM)
        scores = dot(stacked(mine), keys[:, head], NT)
        dprobs = dot(stacked(upstream[:, columns(h)]), values[:, head], NT)
        dscores = []
        for j in range(GROUP):
            for row in range(0, tokens, CHUNK):
                at = slice(j * tokens + row, j * tokens + row + CHUNK)
                masked = scores[at] * SCALE + bias[micro, row : row + CHUNK]
                expo = jnp.exp(masked - jnp.max(masked, axis=-1, keepdims=True))
                probs = expo * (1.0 / jnp.sum(expo, axis=-1, keepdims=True))
                rounded = probs.astype(jnp.bfloat16).astype(jnp.float32)
                delta = jnp.sum(rounded * dprobs[at], axis=-1, keepdims=True)
                dscores.append((probs * (dprobs[at] - delta) * SCALE).astype(jnp.bfloat16))
            if before is not None:
                pull_back(j, before)
        drot = dot(jnp.concatenate(dscores, axis=0), keys[:, head])
        for j in range(GROUP):
            part = drot[j * tokens : (j + 1) * tokens]
            turned = part * cosine[micro] - pltpu.roll(part, HEAD_DIM // 2, 1) * sine[micro]
            at = slice(j * HEAD_DIM, (j + 1) * HEAD_DIM)
            dq[:, at] = turned.astype(jnp.bfloat16)
        dquery[micro, :, columns(h)] = dq[...]
        middle_sum[...] += dot(dq[...], factor_bt[columns(h), :])

    @pl.when(h == 0)
    def _():
        if first:
            for copy in fetch(h):
                copy.wait()
            project()
            for i in NEEDED_NEXT:
                for copy in stage(i):
                    copy.wait()
            upstream[...] = own[micro]
        attend()

    if first:

        @pl.when((h > 0) & (h + 1 < groups))
        def _():
            for copy in fetch(h + 1):
                copy.start()

    @pl.when((h > 0) & (h < groups))
    def _():
        if first:
            for copy in fetch(h):
                copy.wait()
            project()
        attend(dq[...])

    @pl.when(h == groups)
    def _():
        if first:
            for i in NEEDED_LAST:
                for copy in stage(i):
                    copy.wait()
        for piece in range(GROUP):
            pull_back(piece, dq[...])
        mid = middle_sum[...].astype(jnp.bfloat16)
        middle[micro] = mid
        dh = (total[...] + dot(mid, factor_a[...], NT)) * gain[...]
        scaled = rows_in[micro].astype(jnp.float32) * reciprocal[micro]
        mean = jnp.mean(dh * scaled, axis=1, keepdims=True)
        change = reciprocal[micro] * (dh - scaled * mean)
        share = change.shape[1] // len(order)
        for k, i in enumerate(order):
            here = slice(i * share, (i + 1) * share)
            result = upstream[:, here].astype(jnp.float32) + change[:, k * share : (k + 1) * share]
            input_gradient[:, here] = result.astype(jnp.bfloat16)
        grads[0] = input_gradient[...]


def backward(order, step, steps, chosen, staged, weight, incoming, rotated, kept):
    first = step == 0
    own, keys, factor_a = staged[0], staged[3], staged[9]
    micros, tokens, features = own.shape
    width, rank = factor_a.shape
    ctx = keys.shape[0]
    rows = micros * tokens
    block = features // KV_HEADS
    untouched = pl.BlockSpec(memory_space=pl.ANY)
    in_vmem = pl.BlockSpec(memory_space=pltpu.VMEM)
    ins = [(in_hbm(a), untouched) if first else (a, in_vmem) for a in staged]
    ins += [(piece, untouched) for piece in weight] if first else [(weight, in_vmem)]
    if incoming is not None:
        ins.append((incoming, in_vmem))
    if not first:
        ins.append((rotated, in_vmem))
    ins += [(a, in_vmem) for a in kept[:2]] + [(a, untouched) for a in kept[2:]]
    outs = [
        (
            pltpu.HBM((tokens, width), jnp.bfloat16),
            pl.BlockSpec((tokens, width), lambda h, m: (0, 0)),
        ),
        (pltpu.VMEM((micros, tokens, features), jnp.bfloat16), in_vmem),
        (pltpu.VMEM((micros, tokens, rank), jnp.bfloat16), in_vmem),
        (
            pltpu.HBM((micros, tokens, width), jnp.bfloat16),
            pl.BlockSpec((1, tokens, width), lambda h, m: (m[1 + step], 0, 0)),
        ),
    ]
    scratch = [
        pltpu.VMEM((tokens, features), jnp.bfloat16),
        pltpu.VMEM((tokens, block), jnp.bfloat16),
        pltpu.VMEM((tokens, width), jnp.float32),
        pltpu.VMEM((tokens, rank), jnp.float32),
    ]
    if first:
        outs[:0] = [
            (pltpu.VMEM((KV_HEADS, width, block), jnp.bfloat16), in_vmem),
            (pltpu.VMEM((rows, features), jnp.bfloat16), in_vmem),
        ]
        outs += [(pltpu.VMEM(a.shape, a.dtype), in_vmem) for a in staged]
        scratch.append(pltpu.SemaphoreType.DMA((KV_HEADS, len(weight))))
        scratch.append(pltpu.SemaphoreType.DMA((len(staged) + len(order),)))
        aliases = {}
    else:
        outs.append((pltpu.VMEM((KV_HEADS, width, block), jnp.bfloat16), in_vmem))
        at = len(staged)
        aliases = {1 + at: 4, len(ins) - 2: 1, len(ins) - 1: 2, len(ins): 3}
    return pl.pallas_call(
        functools.partial(step_kernel, order, step, steps),
        grid_spec=pltpu.PrefetchScalarGridSpec(
            num_scalar_prefetch=1,
            grid=(KV_HEADS + 1,),
            in_specs=[spec for _, spec in ins],
            out_specs=[spec for _, spec in outs],
            scratch_shapes=scratch,
        ),
        out_shape=[shape for shape, _ in outs],
        input_output_aliases=aliases,
        compiler_params=pltpu.CompilerParams(vmem_limit_bytes=12 * 2**20),
        cost_estimate=pl.CostEstimate(
            flops=2 * tokens * features * (width + 3 * ctx),
            bytes_accessed=2 * width * features,
            transcendentals=tokens * HEADS * ctx,
        ),
        name="first_step" if first else "step",
    )(chosen, *(a for a, _ in ins))


def gradients_kernel(order, normed, middle, dquery, lowrank, out):
    flat = lambda ref: ref[...].reshape(normed.shape[0], ref.shape[-1])
    of_a = dot(flat(middle), normed[...], TN)
    of_bt = dot(lowrank[...], flat(dquery), TN)
    rank = of_a.shape[0]
    share = of_a.shape[1] // len(order)
    lanes = out.shape[2]
    for k, i in enumerate(order):
        for to, top, value in ((i, 0, of_a), (k, rank, of_bt)):
            mine = value[:, k * share : (k + 1) * share].astype(out.dtype)
            if share <= lanes:
                out[to, top : top + rank, :] = mine
                continue
            out[to, top : top + rank, :] = mine[:, :lanes]
            over = share - lanes
            side = lanes // over
            deep = rank // side
            folded = [mine[n * deep : (n + 1) * deep, lanes:] for n in range(side)]
            low = 2 * rank + top // side
            out[to, low : low + deep, :] = jnp.concatenate(folded, axis=1)


def gradients(order, normed, middle, dquery, lowrank):
    rows, width = normed.shape
    rank = middle.shape[-1]
    count = len(order)
    share = width // count
    lanes = min(share, HEAD_DIM)
    deep = 2 * rank * share // lanes
    return pl.pallas_call(
        functools.partial(gradients_kernel, order),
        in_specs=[pl.BlockSpec(memory_space=pltpu.VMEM)] * 4,
        out_shape=jax.ShapeDtypeStruct((count, deep, lanes), jnp.bfloat16),
        compiler_params=pltpu.CompilerParams(vmem_limit_bytes=12 * 2**20),
        name="gradients",
    )(normed, middle, dquery, lowrank)


def unfolded(total, rank, share):
    lanes = total.shape[1]
    if share == lanes:
        return total
    over = share - lanes
    side = lanes // over
    deep = rank // side
    parts = []
    for top in (0, rank):
        low = 2 * rank + top // side
        folded = total[low : low + deep]
        parts.append(
            jnp.concatenate([folded[:, n * over : (n + 1) * over] for n in range(side)], axis=0)
        )
    return jnp.concatenate([total[: 2 * rank], jnp.concatenate(parts, axis=0)], axis=1)


def gather_small(adapter_a, adapter_bt, norm_gain, order):
    count = lax.axis_size("dp")
    packed = jnp.concatenate([adapter_a, adapter_bt, norm_gain[:, None]], axis=1)
    sent = jnp.broadcast_to(packed[None], (count, *packed.shape))
    return lax.all_to_all(
        sent, "dp", split_axis=0, concat_axis=0, tiled=True, axis_index_groups=[order]
    )


def per_device(
    layer_inputs,
    top_grad,
    keys,
    values,
    query_weight,
    adapter_a,
    adapter_bt,
    norm_gain,
    offsets,
    segments,
):
    order = ring_order(lax.axis_size("dp"))
    _, _, micros, tokens, width = layer_inputs.shape
    rows = micros * tokens
    ctx = keys.shape[2]
    keys, values = keys[0, 0], values[0, 0]
    features = query_weight.shape[2]
    rank = adapter_a.shape[2]

    small = gather_small(adapter_a[0], adapter_bt[0], norm_gain[0], order)
    rows_in = reordered(layer_inputs[0, 0], order)
    flat = rows_in.reshape(rows, width).astype(jnp.float32)
    reciprocal = lax.rsqrt(jnp.mean(flat * flat, axis=1, keepdims=True) + norm_eps)

    def make_late(given):
        small, rows_in, reciprocal = given
        factor_bt = small[:, :, rank : 2 * rank].reshape(features, rank)
        factor_a = small[:, :, :rank].reshape(width, rank)
        gain = small[:, :, 2 * rank].reshape(1, width).astype(jnp.float32)
        flat = rows_in.reshape(rows, width).astype(jnp.float32)
        normed = (flat * reciprocal * gain).astype(jnp.bfloat16)
        lowrank = dot(normed, factor_a).astype(jnp.bfloat16)
        return normed, lowrank, factor_bt, factor_a, gain

    positions = (
        offsets[0][:, None] + jnp.arange(tokens, dtype=jnp.int32)[None, :]
    ).reshape(rows)
    seg_row = segments[0]
    place = jnp.arange(ctx, dtype=jnp.int32)
    query_seg = jnp.take(seg_row, positions)
    visible = (place[None, :] <= positions[:, None]) & (
        (seg_row[None, :] == 0) | (seg_row[None, :] == query_seg[:, None])
    )
    bias = jnp.where(visible, 0.0, -1e30).astype(jnp.float32)
    cosine, sine = rope_tables(positions)

    by_micro = lambda a: a.reshape(micros, tokens, a.shape[-1])
    section_count = lax.axis_size("pipe")
    section = lax.axis_index("pipe")
    last = section_count - 1
    steps = 2 * last + micros
    kept, arrived, rotated = (), [], None
    micro = jnp.clip(jnp.arange(steps) - 2 * (last - section), 0, micros - 1)
    is_last = jnp.reshape(section == last, 1).astype(jnp.int32)
    chosen = jnp.concatenate([is_last, micro.astype(jnp.int32), places_of(order)])
    given = small, rows_in, reciprocal
    early = (chosen, *map(by_micro, (bias, cosine, sine, reciprocal)))
    weight, early, late = weight_pieces(query_weight[0], order, early, given, make_late)
    chosen, bias, cosine, sine, reciprocal = early
    normed, lowrank, factor_bt, factor_a, gain = late
    staged = [
        top_grad[0],
        normed,
        lowrank,
        keys,
        values,
        bias,
        cosine,
        sine,
        factor_bt,
        factor_a,
        rows_in,
        reciprocal,
        gain,
    ]
    for step in range(steps):
        incoming = arrived[step - 2] if step >= 2 else None
        made = list(backward(order, step, steps, chosen, staged, weight, incoming, rotated, kept))
        if rotated is None:
            weight, rotated = made.pop(0), made.pop(0)
            made, staged = made[:4], made[4:]
        else:
            weight = made.pop()
        result, *kept = made
        if step < steps - 2:
            arrived.append(
                lax.ppermute(result, "pipe", [(s, s - 1) for s in range(1, section_count)])
            )

    grads = kept[2]
    partial = gradients(order, staged[1], kept[1], kept[0], staged[2])
    got = lax.all_to_all(partial, "dp", split_axis=0, concat_axis=0, tiled=True)
    total = unfolded(jnp.sum(got.astype(jnp.float32), axis=0), rank, width // len(order))
    return (grads[None, None], total[:rank].T[None], total[rank:].T[None])


def solution(mesh):
    placed = (
        P("pipe", "dp", None, None, None),
        P("dp", None, None, None),
        P("pipe", "dp", None, None),
        P("pipe", "dp", None, None),
        P("pipe", "dp", None),
        P("pipe", "dp", None),
        P("pipe", "dp", None),
        P("pipe", "dp"),
        P("dp", None),
        P("dp", None),
    )
    return jax.shard_map(
        per_device,
        mesh=mesh,
        in_specs=placed,
        out_specs=(
            P("pipe", "dp", None, None, None),
            P("pipe", "dp", None),
            P("pipe", "dp", None),
        ),
        check_vma=False,
    )
```

```python
import functools

import jax
import jax.numpy as jnp
from jax import lax
from jax.experimental import pallas as pl
from jax.experimental.pallas import tpu as pltpu
from jax.sharding import PartitionSpec as P

HEADS = 20
KV_HEADS = 4
HEAD_DIM = 128
GROUP = HEADS // KV_HEADS
CHUNK = 16

norm_eps = 1e-06
rope_base = 1000000.0
SCALE = 1.0 / HEAD_DIM**0.5

NT = (((1,), (1,)), ((), ()))
TN = (((0,), (0,)), ((), ()))


def dot(a, b, dims=(((1,), (0,)), ((), ()))):
    return lax.dot_general(a, b, dims, preferred_element_type=jnp.float32)


def rope_tables(positions):
    half = HEAD_DIM // 2
    expon = jnp.arange(half, dtype=jnp.float32) * (2.0 / HEAD_DIM)
    inverse = rope_base ** (-expon)
    angles = positions.astype(jnp.float32)[:, None] * inverse[None, :]
    cosine, sine = jnp.cos(angles), jnp.sin(angles)
    return (
        jnp.concatenate([cosine, cosine], axis=1),
        jnp.concatenate([-sine, sine], axis=1),
    )


def ring_order(count):
    if count % 4:
        return list(range(count))
    chips = count // 2
    columns = 2 ** ((chips.bit_length() - 1) // 2)
    lines = chips // columns
    walk = [(z, 0) for z in range(lines)]
    for step, z in enumerate(range(lines - 1, -1, -1)):
        side = range(1, columns) if step % 2 == 0 else range(columns - 1, 0, -1)
        walk += [(z, x) for x in side]
    return [(z * columns + x) * 2 + core for z, x in walk for core in range(2)]


def reordered(value, order):
    share = value.shape[-1] // len(order)
    return jnp.concatenate(
        [value[..., i * share : (i + 1) * share] for i in order], axis=-1
    )


def stacked(value):
    return jnp.concatenate(
        [value[:, j * HEAD_DIM : (j + 1) * HEAD_DIM] for j in range(GROUP)], axis=0
    )


NEEDED_FIRST = (1, 2, 8, 6, 7)
NEEDED_NEXT = (0, 3, 4, 5)
NEEDED_LAST = (9, 10, 11, 12)
OF_FEATURES = 8


def in_hbm(value):
    return pltpu.with_memory_space_constraint(value, pltpu.HBM)


def places_of(order):
    count = len(order)
    if count != 16:
        return jnp.zeros((1,), jnp.int32)
    chips = count // 2
    table = jnp.array([order.index(i) for i in range(count)], jnp.int32)
    hops = [0]
    for hop in range(1, chips // 2 + 1):
        hops += [-hop, hop] if hop <= (chips - 1) // 2 else [-hop]
    own = (table[lax.axis_index("dp")] + 2 * jnp.array(hops, jnp.int32)) % count
    return jnp.concatenate([own, own ^ 1])


def weight_pieces(shard, order, early, small, make_late):
    count = len(order)
    if count != 16:
        whole = lax.all_gather(shard, "dp", axis=0, tiled=True, axis_index_groups=[order])
        return [whole], early, make_late(small)
    chips = count // 2
    ahead = [
        (order[2 * k + core], order[2 * ((k + 1) % chips) + core])
        for k in range(chips)
        for core in range(2)
    ]
    behind = [(to, source) for source, to in ahead]
    pair = [(i, i ^ 1) for i in range(count)]
    pieces = [shard]
    forward = backward = shard
    for hop in range(1, chips // 2 + 1):
        if hop == 2:
            forward, backward, early = lax.optimization_barrier((forward, backward, early))
        if hop == 3:
            late = make_late(lax.optimization_barrier((small, forward))[0])
        forward = lax.ppermute(forward, "dp", ahead)
        pieces.append(forward)
        if hop <= (chips - 1) // 2:
            backward = lax.ppermute(backward, "dp", behind)
            pieces.append(backward)
    copied = list(pieces)
    copied[-2], late = lax.optimization_barrier((copied[-2], late))
    pieces += [lax.ppermute(piece, "dp", pair) for piece in copied]
    return pieces, early, late


def step_kernel(order, step, steps, chosen, *refs):
    first = step == 0
    refs = list(refs)
    given = arrays = refs[:13]
    incoming = refs[14] if step >= 2 else None
    if first:
        pieces = refs[13:-25]
        held, rotated, input_gradient, dquery, middle, grads = refs[-25:-19]
        staged = refs[-19:-6]
        sems, stage_sems = refs[-2:]
        upstream, dq, total, middle_sum = refs[-6:-2]
        arrays = staged

        def stage(i):
            if i != OF_FEATURES:
                return [pltpu.make_async_copy(given[i], staged[i], stage_sems.at[i])]
            share = given[i].shape[0] // len(order)
            return [
                pltpu.make_async_copy(
                    given[i].at[k * share : (k + 1) * share],
                    staged[i].at[to * share : (to + 1) * share],
                    stage_sems.at[len(given) + k],
                )
                for k, to in enumerate(order)
            ]

    else:
        held = refs[13]
        rotated = refs[14 + (step >= 2)]
        input_gradient, dquery, middle, grads = refs[-9:-5]
        upstream, dq, total, middle_sum = refs[-4:]
    own, normed, lowrank, keys, values, bias, cosine, sine = arrays[:8]
    factor_bt, factor_a, rows_in, reciprocal, gain = arrays[8:]
    h = pl.program_id(0)
    groups = pl.num_programs(0) - 1
    micro = chosen[1 + step]
    tokens = bias.shape[1]
    width = gain.shape[1]
    block = GROUP * HEAD_DIM
    columns = lambda g: pl.ds(pl.multiple_of(g * block, HEAD_DIM), block)

    def fetch(g):
        copies = []
        for i, piece in enumerate(pieces):
            share = piece.shape[0]
            place = chosen[1 + steps + i] if len(pieces) > 1 else 0
            rows = pl.ds(pl.multiple_of(place * share, share), share)
            copies.append(
                pltpu.make_async_copy(
                    piece.at[:, columns(g)], held.at[g, rows, :], sems.at[g, i]
                )
            )
        return copies


    @pl.when(h == 0)
    def _():
        if first:
            for i in NEEDED_FIRST:
                for copy in stage(i):
                    copy.start()
            for copy in fetch(0):
                copy.start()
            for i in NEEDED_NEXT:
                for copy in stage(i):
                    copy.start()
            for copy in fetch(1):
                copy.start()
            for i in NEEDED_LAST:
                for copy in stage(i):
                    copy.start()
            for i in NEEDED_FIRST:
                for copy in stage(i):
                    copy.wait()
        total[...] = jnp.zeros_like(total)
        middle_sum[...] = jnp.zeros_like(middle_sum)
        if first:
            pass
        elif incoming is None:
            upstream[...] = own[micro]
        else:
            is_last = chosen[0] == 1
            upstream[...] = jnp.where(is_last, own[micro], incoming[...])

    def project():
        query = dot(normed[...], held[h]) + dot(lowrank[...], factor_bt[columns(h), :], NT)
        for m in range(rotated.shape[0] // tokens):
            rows = slice(m * tokens, (m + 1) * tokens)
            for j in range(GROUP):
                part = query[rows, j * HEAD_DIM : (j + 1) * HEAD_DIM]
                turned = part * cosine[m] + pltpu.roll(part, HEAD_DIM // 2, 1) * sine[m]
                at = pl.ds(pl.multiple_of(h * block + j * HEAD_DIM, HEAD_DIM), HEAD_DIM)
                rotated[rows, at] = turned.astype(jnp.bfloat16)

    def pull_back(piece, before):
        at = slice(piece * (width // GROUP), (piece + 1) * (width // GROUP))
        total[:, at] += dot(before, held[h - 1, at, :], NT)

    def attend(before=None):
        mine = rotated[pl.ds(pl.multiple_of(micro * tokens, tokens), tokens), columns(h)]
        head = pl.ds(pl.multiple_of(h * HEAD_DIM, HEAD_DIM), HEAD_DIM)
        scores = dot(stacked(mine), keys[:, head], NT)
        dprobs = dot(stacked(upstream[:, columns(h)]), values[:, head], NT)
        dscores = []
        for j in range(GROUP):
            for row in range(0, tokens, CHUNK):
                at = slice(j * tokens + row, j * tokens + row + CHUNK)
                masked = scores[at] * SCALE + bias[micro, row : row + CHUNK]
                expo = jnp.exp(masked - jnp.max(masked, axis=-1, keepdims=True))
                probs = expo * (1.0 / jnp.sum(expo, axis=-1, keepdims=True))
                rounded = probs.astype(jnp.bfloat16).astype(jnp.float32)
                delta = jnp.sum(rounded * dprobs[at], axis=-1, keepdims=True)
                dscores.append((probs * (dprobs[at] - delta) * SCALE).astype(jnp.bfloat16))
            if before is not None:
                pull_back(j, before)
        drot = dot(jnp.concatenate(dscores, axis=0), keys[:, head])
        for j in range(GROUP):
            part = drot[j * tokens : (j + 1) * tokens]
            turned = part * cosine[micro] - pltpu.roll(part, HEAD_DIM // 2, 1) * sine[micro]
            at = slice(j * HEAD_DIM, (j + 1) * HEAD_DIM)
            dq[:, at] = turned.astype(jnp.bfloat16)
        dquery[micro, :, columns(h)] = dq[...]
        middle_sum[...] += dot(dq[...], factor_bt[columns(h), :])

    @pl.when(h == 0)
    def _():
        if first:
            for copy in fetch(h):
                copy.wait()
            project()
            for i in NEEDED_NEXT:
                for copy in stage(i):
                    copy.wait()
            upstream[...] = own[micro]
        attend()

    if first:

        @pl.when((h > 0) & (h + 1 < groups))
        def _():
            for copy in fetch(h + 1):
                copy.start()

    @pl.when((h > 0) & (h < groups))
    def _():
        if first:
            for copy in fetch(h):
                copy.wait()
            project()
        attend(dq[...])

    @pl.when(h == groups)
    def _():
        if first:
            for i in NEEDED_LAST:
                for copy in stage(i):
                    copy.wait()
        for piece in range(GROUP):
            pull_back(piece, dq[...])
        mid = middle_sum[...].astype(jnp.bfloat16)
        middle[micro] = mid
        dh = (total[...] + dot(mid, factor_a[...], NT)) * gain[...]
        scaled = rows_in[micro].astype(jnp.float32) * reciprocal[micro]
        mean = jnp.mean(dh * scaled, axis=1, keepdims=True)
        change = reciprocal[micro] * (dh - scaled * mean)
        share = change.shape[1] // len(order)
        for k, i in enumerate(order):
            here = slice(i * share, (i + 1) * share)
            result = upstream[:, here].astype(jnp.float32) + change[:, k * share : (k + 1) * share]
            input_gradient[:, here] = result.astype(jnp.bfloat16)
        grads[0] = input_gradient[...]


def backward(order, step, steps, chosen, staged, weight, incoming, rotated, kept):
    first = step == 0
    own, keys, factor_a = staged[0], staged[3], staged[9]
    micros, tokens, features = own.shape
    width, rank = factor_a.shape
    ctx = keys.shape[0]
    rows = micros * tokens
    block = features // KV_HEADS
    untouched = pl.BlockSpec(memory_space=pl.ANY)
    in_vmem = pl.BlockSpec(memory_space=pltpu.VMEM)
    ins = [(in_hbm(a), untouched) if first else (a, in_vmem) for a in staged]
    ins += [(in_hbm(a), untouched) for a in weight] if first else [(weight, in_vmem)]
    if incoming is not None:
        ins.append((incoming, in_vmem))
    if not first:
        ins.append((rotated, in_vmem))
    ins += [(a, in_vmem) for a in kept[:2]] + [(a, untouched) for a in kept[2:]]
    outs = [
        (
            pltpu.HBM((tokens, width), jnp.bfloat16),
            pl.BlockSpec((tokens, width), lambda h, m: (0, 0)),
        ),
        (pltpu.VMEM((micros, tokens, features), jnp.bfloat16), in_vmem),
        (pltpu.VMEM((micros, tokens, rank), jnp.bfloat16), in_vmem),
        (
            pltpu.HBM((micros, tokens, width), jnp.bfloat16),
            pl.BlockSpec((1, tokens, width), lambda h, m: (m[1 + step], 0, 0)),
        ),
    ]
    scratch = [
        pltpu.VMEM((tokens, features), jnp.bfloat16),
        pltpu.VMEM((tokens, block), jnp.bfloat16),
        pltpu.VMEM((tokens, width), jnp.float32),
        pltpu.VMEM((tokens, rank), jnp.float32),
    ]
    if first:
        outs[:0] = [
            (pltpu.VMEM((KV_HEADS, width, block), jnp.bfloat16), in_vmem),
            (pltpu.VMEM((rows, features), jnp.bfloat16), in_vmem),
        ]
        outs += [(pltpu.VMEM(a.shape, a.dtype), in_vmem) for a in staged]
        scratch.append(pltpu.SemaphoreType.DMA((KV_HEADS, len(weight))))
        scratch.append(pltpu.SemaphoreType.DMA((len(staged) + len(order),)))
        aliases = {}
    else:
        outs.append((pltpu.VMEM((KV_HEADS, width, block), jnp.bfloat16), in_vmem))
        at = len(staged)
        aliases = {1 + at: 4, len(ins) - 2: 1, len(ins) - 1: 2, len(ins): 3}
    return pl.pallas_call(
        functools.partial(step_kernel, order, step, steps),
        grid_spec=pltpu.PrefetchScalarGridSpec(
            num_scalar_prefetch=1,
            grid=(KV_HEADS + 1,),
            in_specs=[spec for _, spec in ins],
            out_specs=[spec for _, spec in outs],
            scratch_shapes=scratch,
        ),
        out_shape=[shape for shape, _ in outs],
        input_output_aliases=aliases,
        compiler_params=pltpu.CompilerParams(vmem_limit_bytes=12 * 2**20),
        cost_estimate=pl.CostEstimate(
            flops=2 * tokens * features * (width + 3 * ctx),
            bytes_accessed=2 * width * features,
            transcendentals=tokens * HEADS * ctx,
        ),
        name="first_step" if first else "step",
    )(chosen, *(a for a, _ in ins))


def gradients_kernel(order, normed, middle, dquery, lowrank, out):
    flat = lambda ref: ref[...].reshape(normed.shape[0], ref.shape[-1])
    of_a = dot(flat(middle), normed[...], TN)
    of_bt = dot(lowrank[...], flat(dquery), TN)
    rank = of_a.shape[0]
    share = of_a.shape[1] // len(order)
    lanes = out.shape[2]
    for k, i in enumerate(order):
        for to, top, value in ((i, 0, of_a), (k, rank, of_bt)):
            mine = value[:, k * share : (k + 1) * share].astype(out.dtype)
            if share <= lanes:
                out[to, top : top + rank, :] = mine
                continue
            out[to, top : top + rank, :] = mine[:, :lanes]
            over = share - lanes
            side = lanes // over
            deep = rank // side
            folded = [mine[n * deep : (n + 1) * deep, lanes:] for n in range(side)]
            low = 2 * rank + top // side
            out[to, low : low + deep, :] = jnp.concatenate(folded, axis=1)


def gradients(order, normed, middle, dquery, lowrank):
    rows, width = normed.shape
    rank = middle.shape[-1]
    count = len(order)
    share = width // count
    lanes = min(share, HEAD_DIM)
    deep = 2 * rank * share // lanes
    return pl.pallas_call(
        functools.partial(gradients_kernel, order),
        in_specs=[pl.BlockSpec(memory_space=pltpu.VMEM)] * 4,
        out_shape=jax.ShapeDtypeStruct((count, deep, lanes), jnp.bfloat16),
        compiler_params=pltpu.CompilerParams(vmem_limit_bytes=12 * 2**20),
        name="gradients",
    )(normed, middle, dquery, lowrank)


def unfolded(total, rank, share):
    lanes = total.shape[1]
    if share == lanes:
        return total
    over = share - lanes
    side = lanes // over
    deep = rank // side
    parts = []
    for top in (0, rank):
        low = 2 * rank + top // side
        folded = total[low : low + deep]
        parts.append(
            jnp.concatenate([folded[:, n * over : (n + 1) * over] for n in range(side)], axis=0)
        )
    return jnp.concatenate([total[: 2 * rank], jnp.concatenate(parts, axis=0)], axis=1)


def gather_small(adapter_a, adapter_bt, norm_gain, order):
    count = lax.axis_size("dp")
    packed = jnp.concatenate([adapter_a, adapter_bt, norm_gain[:, None]], axis=1)
    sent = jnp.broadcast_to(packed[None], (count, *packed.shape))
    return lax.all_to_all(
        sent, "dp", split_axis=0, concat_axis=0, tiled=True, axis_index_groups=[order]
    )


def per_device(
    layer_inputs,
    top_grad,
    keys,
    values,
    query_weight,
    adapter_a,
    adapter_bt,
    norm_gain,
    offsets,
    segments,
):
    order = ring_order(lax.axis_size("dp"))
    _, _, micros, tokens, width = layer_inputs.shape
    rows = micros * tokens
    ctx = keys.shape[2]
    keys, values = keys[0, 0], values[0, 0]
    features = query_weight.shape[2]
    rank = adapter_a.shape[2]

    small = gather_small(adapter_a[0], adapter_bt[0], norm_gain[0], order)
    rows_in = reordered(layer_inputs[0, 0], order)
    flat = rows_in.reshape(rows, width).astype(jnp.float32)
    reciprocal = lax.rsqrt(jnp.mean(flat * flat, axis=1, keepdims=True) + norm_eps)

    def make_late(given):
        small, rows_in, reciprocal = given
        factor_bt = small[:, :, rank : 2 * rank].reshape(features, rank)
        factor_a = small[:, :, :rank].reshape(width, rank)
        gain = small[:, :, 2 * rank].reshape(1, width).astype(jnp.float32)
        flat = rows_in.reshape(rows, width).astype(jnp.float32)
        normed = (flat * reciprocal * gain).astype(jnp.bfloat16)
        lowrank = dot(normed, factor_a).astype(jnp.bfloat16)
        return normed, lowrank, factor_bt, factor_a, gain

    positions = (
        offsets[0][:, None] + jnp.arange(tokens, dtype=jnp.int32)[None, :]
    ).reshape(rows)
    seg_row = segments[0]
    place = jnp.arange(ctx, dtype=jnp.int32)
    query_seg = jnp.take(seg_row, positions)
    visible = (place[None, :] <= positions[:, None]) & (
        (seg_row[None, :] == 0) | (seg_row[None, :] == query_seg[:, None])
    )
    bias = jnp.where(visible, 0.0, -1e30).astype(jnp.float32)
    cosine, sine = rope_tables(positions)

    by_micro = lambda a: a.reshape(micros, tokens, a.shape[-1])
    section_count = lax.axis_size("pipe")
    section = lax.axis_index("pipe")
    last = section_count - 1
    steps = 2 * last + micros
    kept, arrived, rotated = (), [], None
    micro = jnp.clip(jnp.arange(steps) - 2 * (last - section), 0, micros - 1)
    is_last = jnp.reshape(section == last, 1).astype(jnp.int32)
    chosen = jnp.concatenate([is_last, micro.astype(jnp.int32), places_of(order)])
    given = small, rows_in, reciprocal
    early = (chosen, *map(by_micro, (bias, cosine, sine, reciprocal)))
    weight, early, late = weight_pieces(query_weight[0], order, early, given, make_late)
    chosen, bias, cosine, sine, reciprocal = early
    normed, lowrank, factor_bt, factor_a, gain = late
    staged = [
        top_grad[0],
        normed,
        lowrank,
        keys,
        values,
        bias,
        cosine,
        sine,
        factor_bt,
        factor_a,
        rows_in,
        reciprocal,
        gain,
    ]
    for step in range(steps):
        incoming = arrived[step - 2] if step >= 2 else None
        made = list(backward(order, step, steps, chosen, staged, weight, incoming, rotated, kept))
        if rotated is None:
            weight, rotated = made.pop(0), made.pop(0)
            made, staged = made[:4], made[4:]
        else:
            weight = made.pop()
        result, *kept = made
        if step < steps - 2:
            arrived.append(
                lax.ppermute(result, "pipe", [(s, s - 1) for s in range(1, section_count)])
            )

    grads = kept[2]
    partial = gradients(order, staged[1], kept[1], kept[0], staged[2])
    got = lax.all_to_all(partial, "dp", split_axis=0, concat_axis=0, tiled=True)
    total = unfolded(jnp.sum(got.astype(jnp.float32), axis=0), rank, width // len(order))
    return (grads[None, None], total[:rank].T[None], total[rank:].T[None])


def solution(mesh):
    placed = (
        P("pipe", "dp", None, None, None),
        P("dp", None, None, None),
        P("pipe", "dp", None, None),
        P("pipe", "dp", None, None),
        P("pipe", "dp", None),
        P("pipe", "dp", None),
        P("pipe", "dp", None),
        P("pipe", "dp"),
        P("dp", None),
        P("dp", None),
    )
    return jax.shard_map(
        per_device,
        mesh=mesh,
        in_specs=placed,
        out_specs=(
            P("pipe", "dp", None, None, None),
            P("pipe", "dp", None),
            P("pipe", "dp", None),
        ),
        check_vma=False,
    )
```

```python
import functools

import jax
import jax.numpy as jnp
from jax import lax
from jax.experimental import pallas as pl
from jax.experimental.pallas import tpu as pltpu
from jax.sharding import PartitionSpec as P

HEADS = 20
KV_HEADS = 4
HEAD_DIM = 128
GROUP = HEADS // KV_HEADS
CHUNK = 16

norm_eps = 1e-06
rope_base = 1000000.0
SCALE = 1.0 / HEAD_DIM**0.5

NT = (((1,), (1,)), ((), ()))
TN = (((0,), (0,)), ((), ()))


def dot(a, b, dims=(((1,), (0,)), ((), ()))):
    return lax.dot_general(a, b, dims, preferred_element_type=jnp.float32)


def rope_tables(positions):
    half = HEAD_DIM // 2
    expon = jnp.arange(half, dtype=jnp.float32) * (2.0 / HEAD_DIM)
    inverse = rope_base ** (-expon)
    angles = positions.astype(jnp.float32)[:, None] * inverse[None, :]
    cosine, sine = jnp.cos(angles), jnp.sin(angles)
    return (
        jnp.concatenate([cosine, cosine], axis=1),
        jnp.concatenate([-sine, sine], axis=1),
    )


def ring_order(count):
    if count % 4:
        return list(range(count))
    chips = count // 2
    columns = 2 ** ((chips.bit_length() - 1) // 2)
    lines = chips // columns
    walk = [(z, 0) for z in range(lines)]
    for step, z in enumerate(range(lines - 1, -1, -1)):
        side = range(1, columns) if step % 2 == 0 else range(columns - 1, 0, -1)
        walk += [(z, x) for x in side]
    return [(z * columns + x) * 2 + core for z, x in walk for core in range(2)]


def reordered(value, order):
    share = value.shape[-1] // len(order)
    return jnp.concatenate(
        [value[..., i * share : (i + 1) * share] for i in order], axis=-1
    )


def stacked(value):
    return jnp.concatenate(
        [value[:, j * HEAD_DIM : (j + 1) * HEAD_DIM] for j in range(GROUP)], axis=0
    )


NEEDED_FIRST = (1, 2, 8, 6, 7)
NEEDED_NEXT = (0, 3, 4, 5)
NEEDED_LAST = (9, 10, 11, 12)
OF_FEATURES = 8


def in_hbm(value):
    return pltpu.with_memory_space_constraint(value, pltpu.HBM)


def places_of(order):
    count = len(order)
    if count != 16:
        return jnp.zeros((1,), jnp.int32)
    chips = count // 2
    table = jnp.array([order.index(i) for i in range(count)], jnp.int32)
    hops = [0]
    for hop in range(1, chips // 2 + 1):
        hops += [-hop, hop] if hop <= (chips - 1) // 2 else [-hop]
    own = (table[lax.axis_index("dp")] + 2 * jnp.array(hops, jnp.int32)) % count
    return jnp.concatenate([own, own ^ 1])


def weight_pieces(shard, order, early, small, make_late):
    count = len(order)
    if count != 16:
        whole = lax.all_gather(shard, "dp", axis=0, tiled=True, axis_index_groups=[order])
        return [whole], early, make_late(small)
    chips = count // 2
    ahead = [
        (order[2 * k + core], order[2 * ((k + 1) % chips) + core])
        for k in range(chips)
        for core in range(2)
    ]
    behind = [(to, source) for source, to in ahead]
    pair = [(i, i ^ 1) for i in range(count)]
    pieces = [shard]
    forward = backward = shard
    for hop in range(1, chips // 2 + 1):
        if hop == 2:
            forward, backward, early = lax.optimization_barrier((forward, backward, early))
        if hop == 3:
            late = make_late(small)
        forward = lax.ppermute(forward, "dp", ahead)
        pieces.append(forward)
        if hop <= (chips - 1) // 2:
            backward = lax.ppermute(backward, "dp", behind)
            pieces.append(backward)
    copied = list(pieces)
    copied[-2], late = lax.optimization_barrier((copied[-2], late))
    pieces += [lax.ppermute(piece, "dp", pair) for piece in copied]
    return pieces, early, late


def step_kernel(order, step, steps, chosen, *refs):
    first = step == 0
    refs = list(refs)
    given = arrays = refs[:13]
    incoming = refs[14] if step >= 2 else None
    if first:
        pieces = refs[13:-25]
        held, rotated, input_gradient, dquery, middle, grads = refs[-25:-19]
        staged = refs[-19:-6]
        sems, stage_sems = refs[-2:]
        upstream, dq, total, middle_sum = refs[-6:-2]
        arrays = staged

        def stage(i):
            if i != OF_FEATURES:
                return [pltpu.make_async_copy(given[i], staged[i], stage_sems.at[i])]
            share = given[i].shape[0] // len(order)
            return [
                pltpu.make_async_copy(
                    given[i].at[k * share : (k + 1) * share],
                    staged[i].at[to * share : (to + 1) * share],
                    stage_sems.at[len(given) + k],
                )
                for k, to in enumerate(order)
            ]

    else:
        held = refs[13]
        rotated = refs[14 + (step >= 2)]
        input_gradient, dquery, middle, grads = refs[-9:-5]
        upstream, dq, total, middle_sum = refs[-4:]
    own, normed, lowrank, keys, values, bias, cosine, sine = arrays[:8]
    factor_bt, factor_a, rows_in, reciprocal, gain = arrays[8:]
    h = pl.program_id(0)
    groups = pl.num_programs(0) - 1
    micro = chosen[1 + step]
    tokens = bias.shape[1]
    width = gain.shape[1]
    block = GROUP * HEAD_DIM
    columns = lambda g: pl.ds(pl.multiple_of(g * block, HEAD_DIM), block)

    def fetch(g):
        copies = []
        for i, piece in enumerate(pieces):
            share = piece.shape[0]
            place = chosen[1 + steps + i] if len(pieces) > 1 else 0
            rows = pl.ds(pl.multiple_of(place * share, share), share)
            copies.append(
                pltpu.make_async_copy(
                    piece.at[:, columns(g)], held.at[g, rows, :], sems.at[g, i]
                )
            )
        return copies


    @pl.when(h == 0)
    def _():
        if first:
            for i in NEEDED_FIRST:
                for copy in stage(i):
                    copy.start()
            for copy in fetch(0):
                copy.start()
            for i in NEEDED_NEXT:
                for copy in stage(i):
                    copy.start()
            for copy in fetch(1):
                copy.start()
            for i in NEEDED_LAST:
                for copy in stage(i):
                    copy.start()
            for i in NEEDED_FIRST:
                for copy in stage(i):
                    copy.wait()
        total[...] = jnp.zeros_like(total)
        middle_sum[...] = jnp.zeros_like(middle_sum)
        if first:
            pass
        elif incoming is None:
            upstream[...] = own[micro]
        else:
            is_last = chosen[0] == 1
            upstream[...] = jnp.where(is_last, own[micro], incoming[...])

    def project():
        query = dot(normed[...], held[h]) + dot(lowrank[...], factor_bt[columns(h), :], NT)
        for m in range(rotated.shape[0] // tokens):
            rows = slice(m * tokens, (m + 1) * tokens)
            for j in range(GROUP):
                part = query[rows, j * HEAD_DIM : (j + 1) * HEAD_DIM]
                turned = part * cosine[m] + pltpu.roll(part, HEAD_DIM // 2, 1) * sine[m]
                at = pl.ds(pl.multiple_of(h * block + j * HEAD_DIM, HEAD_DIM), HEAD_DIM)
                rotated[rows, at] = turned.astype(jnp.bfloat16)

    def pull_back(piece, before):
        at = slice(piece * (width // GROUP), (piece + 1) * (width // GROUP))
        total[:, at] += dot(before, held[h - 1, at, :], NT)

    def attend(before=None):
        mine = rotated[pl.ds(pl.multiple_of(micro * tokens, tokens), tokens), columns(h)]
        head = pl.ds(pl.multiple_of(h * HEAD_DIM, HEAD_DIM), HEAD_DIM)
        scores = dot(stacked(mine), keys[:, head], NT)
        dprobs = dot(stacked(upstream[:, columns(h)]), values[:, head], NT)
        dscores = []
        for j in range(GROUP):
            for row in range(0, tokens, CHUNK):
                at = slice(j * tokens + row, j * tokens + row + CHUNK)
                masked = scores[at] * SCALE + bias[micro, row : row + CHUNK]
                expo = jnp.exp(masked - jnp.max(masked, axis=-1, keepdims=True))
                probs = expo * (1.0 / jnp.sum(expo, axis=-1, keepdims=True))
                rounded = probs.astype(jnp.bfloat16).astype(jnp.float32)
                delta = jnp.sum(rounded * dprobs[at], axis=-1, keepdims=True)
                dscores.append((probs * (dprobs[at] - delta) * SCALE).astype(jnp.bfloat16))
            if before is not None:
                pull_back(j, before)
        drot = dot(jnp.concatenate(dscores, axis=0), keys[:, head])
        for j in range(GROUP):
            part = drot[j * tokens : (j + 1) * tokens]
            turned = part * cosine[micro] - pltpu.roll(part, HEAD_DIM // 2, 1) * sine[micro]
            at = slice(j * HEAD_DIM, (j + 1) * HEAD_DIM)
            dq[:, at] = turned.astype(jnp.bfloat16)
        dquery[micro, :, columns(h)] = dq[...]
        middle_sum[...] += dot(dq[...], factor_bt[columns(h), :])

    @pl.when(h == 0)
    def _():
        if first:
            for copy in fetch(h):
                copy.wait()
            project()
            for i in NEEDED_NEXT:
                for copy in stage(i):
                    copy.wait()
            upstream[...] = own[micro]
        attend()

    if first:

        @pl.when((h > 0) & (h + 1 < groups))
        def _():
            for copy in fetch(h + 1):
                copy.start()

    @pl.when((h > 0) & (h < groups))
    def _():
        if first:
            for copy in fetch(h):
                copy.wait()
            project()
        attend(dq[...])

    @pl.when(h == groups)
    def _():
        if first:
            for i in NEEDED_LAST:
                for copy in stage(i):
                    copy.wait()
        for piece in range(GROUP):
            pull_back(piece, dq[...])
        mid = middle_sum[...].astype(jnp.bfloat16)
        middle[micro] = mid
        dh = (total[...] + dot(mid, factor_a[...], NT)) * gain[...]
        scaled = rows_in[micro].astype(jnp.float32) * reciprocal[micro]
        mean = jnp.mean(dh * scaled, axis=1, keepdims=True)
        change = reciprocal[micro] * (dh - scaled * mean)
        share = change.shape[1] // len(order)
        for k, i in enumerate(order):
            here = slice(i * share, (i + 1) * share)
            result = upstream[:, here].astype(jnp.float32) + change[:, k * share : (k + 1) * share]
            input_gradient[:, here] = result.astype(jnp.bfloat16)
        grads[0] = input_gradient[...]


def backward(order, step, steps, chosen, staged, weight, incoming, rotated, kept):
    first = step == 0
    own, keys, factor_a = staged[0], staged[3], staged[9]
    micros, tokens, features = own.shape
    width, rank = factor_a.shape
    ctx = keys.shape[0]
    rows = micros * tokens
    block = features // KV_HEADS
    untouched = pl.BlockSpec(memory_space=pl.ANY)
    in_vmem = pl.BlockSpec(memory_space=pltpu.VMEM)
    ins = [(in_hbm(a), untouched) if first else (a, in_vmem) for a in staged]
    ins += [(in_hbm(a), untouched) for a in weight] if first else [(weight, in_vmem)]
    if incoming is not None:
        ins.append((incoming, in_vmem))
    if not first:
        ins.append((rotated, in_vmem))
    ins += [(a, in_vmem) for a in kept[:2]] + [(a, untouched) for a in kept[2:]]
    outs = [
        (
            pltpu.HBM((tokens, width), jnp.bfloat16),
            pl.BlockSpec((tokens, width), lambda h, m: (0, 0)),
        ),
        (pltpu.VMEM((micros, tokens, features), jnp.bfloat16), in_vmem),
        (pltpu.VMEM((micros, tokens, rank), jnp.bfloat16), in_vmem),
        (
            pltpu.HBM((micros, tokens, width), jnp.bfloat16),
            pl.BlockSpec((1, tokens, width), lambda h, m: (m[1 + step], 0, 0)),
        ),
    ]
    scratch = [
        pltpu.VMEM((tokens, features), jnp.bfloat16),
        pltpu.VMEM((tokens, block), jnp.bfloat16),
        pltpu.VMEM((tokens, width), jnp.float32),
        pltpu.VMEM((tokens, rank), jnp.float32),
    ]
    if first:
        outs[:0] = [
            (pltpu.VMEM((KV_HEADS, width, block), jnp.bfloat16), in_vmem),
            (pltpu.VMEM((rows, features), jnp.bfloat16), in_vmem),
        ]
        outs += [(pltpu.VMEM(a.shape, a.dtype), in_vmem) for a in staged]
        scratch.append(pltpu.SemaphoreType.DMA((KV_HEADS, len(weight))))
        scratch.append(pltpu.SemaphoreType.DMA((len(staged) + len(order),)))
        aliases = {}
    else:
        outs.append((pltpu.VMEM((KV_HEADS, width, block), jnp.bfloat16), in_vmem))
        at = len(staged)
        aliases = {1 + at: 4, len(ins) - 2: 1, len(ins) - 1: 2, len(ins): 3}
    return pl.pallas_call(
        functools.partial(step_kernel, order, step, steps),
        grid_spec=pltpu.PrefetchScalarGridSpec(
            num_scalar_prefetch=1,
            grid=(KV_HEADS + 1,),
            in_specs=[spec for _, spec in ins],
            out_specs=[spec for _, spec in outs],
            scratch_shapes=scratch,
        ),
        out_shape=[shape for shape, _ in outs],
        input_output_aliases=aliases,
        compiler_params=pltpu.CompilerParams(vmem_limit_bytes=12 * 2**20),
        cost_estimate=pl.CostEstimate(
            flops=2 * tokens * features * (width + 3 * ctx),
            bytes_accessed=2 * width * features,
            transcendentals=tokens * HEADS * ctx,
        ),
        name="first_step" if first else "step",
    )(chosen, *(a for a, _ in ins))


def gradients_kernel(order, normed, middle, dquery, lowrank, out):
    flat = lambda ref: ref[...].reshape(normed.shape[0], ref.shape[-1])
    of_a = dot(flat(middle), normed[...], TN)
    of_bt = dot(lowrank[...], flat(dquery), TN)
    rank = of_a.shape[0]
    share = of_a.shape[1] // len(order)
    lanes = out.shape[2]
    for k, i in enumerate(order):
        for to, top, value in ((i, 0, of_a), (k, rank, of_bt)):
            mine = value[:, k * share : (k + 1) * share].astype(out.dtype)
            if share <= lanes:
                out[to, top : top + rank, :] = mine
                continue
            out[to, top : top + rank, :] = mine[:, :lanes]
            over = share - lanes
            side = lanes // over
            deep = rank // side
            folded = [mine[n * deep : (n + 1) * deep, lanes:] for n in range(side)]
            low = 2 * rank + top // side
            out[to, low : low + deep, :] = jnp.concatenate(folded, axis=1)


def gradients(order, normed, middle, dquery, lowrank):
    rows, width = normed.shape
    rank = middle.shape[-1]
    count = len(order)
    share = width // count
    lanes = min(share, HEAD_DIM)
    deep = 2 * rank * share // lanes
    return pl.pallas_call(
        functools.partial(gradients_kernel, order),
        in_specs=[pl.BlockSpec(memory_space=pltpu.VMEM)] * 4,
        out_shape=jax.ShapeDtypeStruct((count, deep, lanes), jnp.bfloat16),
        compiler_params=pltpu.CompilerParams(vmem_limit_bytes=12 * 2**20),
        name="gradients",
    )(normed, middle, dquery, lowrank)


def unfolded(total, rank, share):
    lanes = total.shape[1]
    if share == lanes:
        return total
    over = share - lanes
    side = lanes // over
    deep = rank // side
    parts = []
    for top in (0, rank):
        low = 2 * rank + top // side
        folded = total[low : low + deep]
        parts.append(
            jnp.concatenate([folded[:, n * over : (n + 1) * over] for n in range(side)], axis=0)
        )
    return jnp.concatenate([total[: 2 * rank], jnp.concatenate(parts, axis=0)], axis=1)


def gather_small(adapter_a, adapter_bt, norm_gain, order):
    count = lax.axis_size("dp")
    packed = jnp.concatenate([adapter_a, adapter_bt, norm_gain[:, None]], axis=1)
    sent = jnp.broadcast_to(packed[None], (count, *packed.shape))
    return lax.all_to_all(
        sent, "dp", split_axis=0, concat_axis=0, tiled=True, axis_index_groups=[order]
    )


def per_device(
    layer_inputs,
    top_grad,
    keys,
    values,
    query_weight,
    adapter_a,
    adapter_bt,
    norm_gain,
    offsets,
    segments,
):
    order = ring_order(lax.axis_size("dp"))
    _, _, micros, tokens, width = layer_inputs.shape
    rows = micros * tokens
    ctx = keys.shape[2]
    keys, values = keys[0, 0], values[0, 0]
    features = query_weight.shape[2]
    rank = adapter_a.shape[2]

    small = gather_small(adapter_a[0], adapter_bt[0], norm_gain[0], order)
    rows_in = reordered(layer_inputs[0, 0], order)
    flat = rows_in.reshape(rows, width).astype(jnp.float32)
    reciprocal = lax.rsqrt(jnp.mean(flat * flat, axis=1, keepdims=True) + norm_eps)

    def make_late(given):
        small, rows_in, reciprocal = given
        factor_bt = small[:, :, rank : 2 * rank].reshape(features, rank)
        factor_a = small[:, :, :rank].reshape(width, rank)
        gain = small[:, :, 2 * rank].reshape(1, width).astype(jnp.float32)
        flat = rows_in.reshape(rows, width).astype(jnp.float32)
        normed = (flat * reciprocal * gain).astype(jnp.bfloat16)
        lowrank = dot(normed, factor_a).astype(jnp.bfloat16)
        return normed, lowrank, factor_bt, factor_a, gain

    positions = (
        offsets[0][:, None] + jnp.arange(tokens, dtype=jnp.int32)[None, :]
    ).reshape(rows)
    seg_row = segments[0]
    place = jnp.arange(ctx, dtype=jnp.int32)
    query_seg = jnp.take(seg_row, positions)
    visible = (place[None, :] <= positions[:, None]) & (
        (seg_row[None, :] == 0) | (seg_row[None, :] == query_seg[:, None])
    )
    bias = jnp.where(visible, 0.0, -1e30).astype(jnp.float32)
    cosine, sine = rope_tables(positions)

    by_micro = lambda a: a.reshape(micros, tokens, a.shape[-1])
    section_count = lax.axis_size("pipe")
    section = lax.axis_index("pipe")
    last = section_count - 1
    steps = 2 * last + micros
    kept, arrived, rotated = (), [], None
    micro = jnp.clip(jnp.arange(steps) - 2 * (last - section), 0, micros - 1)
    is_last = jnp.reshape(section == last, 1).astype(jnp.int32)
    chosen = jnp.concatenate([is_last, micro.astype(jnp.int32), places_of(order)])
    given = small, rows_in, reciprocal
    early = (chosen, *map(by_micro, (bias, cosine, sine, reciprocal)))
    weight, early, late = weight_pieces(query_weight[0], order, early, given, make_late)
    chosen, bias, cosine, sine, reciprocal = early
    normed, lowrank, factor_bt, factor_a, gain = late
    staged = [
        top_grad[0],
        normed,
        lowrank,
        keys,
        values,
        bias,
        cosine,
        sine,
        factor_bt,
        factor_a,
        rows_in,
        reciprocal,
        gain,
    ]
    for step in range(steps):
        incoming = arrived[step - 2] if step >= 2 else None
        made = list(backward(order, step, steps, chosen, staged, weight, incoming, rotated, kept))
        if rotated is None:
            weight, rotated = made.pop(0), made.pop(0)
            made, staged = made[:4], made[4:]
        else:
            weight = made.pop()
        result, *kept = made
        if step < steps - 2:
            arrived.append(
                lax.ppermute(result, "pipe", [(s, s - 1) for s in range(1, section_count)])
            )

    grads = kept[2]
    partial = gradients(order, staged[1], kept[1], kept[0], staged[2])
    got = lax.all_to_all(partial, "dp", split_axis=0, concat_axis=0, tiled=True)
    total = unfolded(jnp.sum(got.astype(jnp.float32), axis=0), rank, width // len(order))
    return (grads[None, None], total[:rank].T[None], total[rank:].T[None])


def solution(mesh):
    placed = (
        P("pipe", "dp", None, None, None),
        P("dp", None, None, None),
        P("pipe", "dp", None, None),
        P("pipe", "dp", None, None),
        P("pipe", "dp", None),
        P("pipe", "dp", None),
        P("pipe", "dp", None),
        P("pipe", "dp"),
        P("dp", None),
        P("dp", None),
    )
    return jax.shard_map(
        per_device,
        mesh=mesh,
        in_specs=placed,
        out_specs=(
            P("pipe", "dp", None, None, None),
            P("pipe", "dp", None),
            P("pipe", "dp", None),
        ),
        check_vma=False,
    )
```
